32 devices in a mesh: grp: 8 (over z, y), tp: 4 (over x, core).
Axes of the slice: x: 2, y: 2, z: 4, core: 2. Of those that a mesh axis runs over, the one named last changes fastest.
Arguments:
- queries: bfloat16 [4096, 4096], P('grp', 'tp'), may hold values from -120 to 120
- keys: bfloat16 [4096, 1024], P('grp', 'tp'), may hold values from -6 to 6
- values: bfloat16 [4096, 1024], P('grp', 'tp'), may hold values from -6 to 6
- segment_ids: int32 [4096], replicated, may hold values from 0 to 31, never falling along the last dimension, each value on 1 to 256 neighbouring positions
- cache_owner: int32 [4096, 1], P('grp'), may hold values from 0 to 7; in each aligned block of 512 rows (0 to 511, 512 to 1023, ...) at most 128 rows name the same one
Outputs:
- attention: bfloat16 [4096, 4096], P('grp', 'tp')
- key_cache: bfloat16 [8192, 1024], P(('grp', 'tp'))
- value_cache: bfloat16 [8192, 1024], P(('grp', 'tp'))
The draws below stay inside these ranges and needn't reach their ends.
Inputs may be any that keep to these rules, and one draw needn't show every extreme that they name: `segment_ids`: ids never fall along the stream; every request has 1 to 256 tokens and one has exactly 256. `cache_owner`: in each aligned block of 512 rows no owner is named more than 128 times, a bound that some block reaches.
All inputs are finite; a program needn't handle non-finite values.
Results may differ from the reference program's by a relative error of at most 0.008.
Values may be sent and summed in bfloat16 or wider, within the bound.
A program may use at most 64 MiB of HBM per device.

```python
import math
import jax
import jax.numpy as jnp
import numpy as np
from jax import lax

HEADS = 32
KV_HEADS = 8
HEAD_DIM = 128
TOK_GRP = 512
TOKENS = 4096
MOST_LEN = 256
SEGMENTS = 32
QCAP = 32
CAP = 128
SLOTS = 1024
N_GRP = 8


def shared_keys(key):
    source = jax.random.fold_in(key, 7)
    return jnp.clip(jax.random.normal(source, (TOKENS, KV_HEADS * HEAD_DIM), jnp.float32), -6.0, 6.0)


def draw_keys(key, part):
    return shared_keys(key).astype(jnp.bfloat16)


def draw_queries(key, part):
    drawn = jnp.clip(jax.random.normal(jax.random.fold_in(key, 3), (TOKENS, HEADS * HEAD_DIM), jnp.float32), -6.0, 6.0)
    return drawn.astype(jnp.bfloat16)


def block_scale(stream_key, shape, pieces, low, top_value):
    def one(axis_at, shards_of):
        draws = jax.random.uniform(jax.random.fold_in(jax.random.fold_in(stream_key, 6), axis_at), (shards_of,), jnp.float32, low / len(pieces), top_value / len(pieces))
        return jnp.repeat(jnp.exp(draws), shape[axis_at] // shards_of).reshape((-1,) + (1,) * (len(shape) - axis_at - 1))

    level = one(*pieces[0])
    for cut in pieces[1:]:
        level = level * one(*cut)
    return level


def split_up(count, total, most, lean):
    portions = [(1 << 20) // math.isqrt(rank ** lean) + 1 for rank in range(2, count + 1)]
    spare, counts = total - most - (count - 1), [1] * (count - 1)
    while spare > 0:
        free = [i for i in range(count - 1) if counts[i] < most]
        whole, left = sum([portions[i] for i in free]), spare
        for i in free:
            more = min(most - counts[i], max(1, left * portions[i] // whole), spare)
            counts[i] = counts[i] + more
            spare = spare - more
    return np.array([most] + counts)


def uneven(rng, count, total, bound, lean):
    if count == 2:
        one = jax.random.randint(rng, (), max(1, total - bound), min(bound, total - 1) + 1)
        return jnp.stack([one, total - one])
    sizes = jnp.asarray(split_up(count, total, bound, lean), jnp.int32)
    couples = (count - 1) // 2
    giver, sink = sizes[1:1 + 2 * couples:2], sizes[2:2 + 2 * couples:2]
    margin = jnp.minimum(giver - 1, bound - sink)
    shifted = jax.random.randint(jax.random.fold_in(rng, 1), (couples,), 0, 1 << 20) % (margin + 1)
    sizes = sizes.at[1:1 + 2 * couples:2].set(giver - shifted).at[2:2 + 2 * couples:2].set(sink + shifted)
    return sizes[jax.random.permutation(jax.random.fold_in(rng, 2), count)]


def deal_out(own_key, own, number, rows, number_of, top, reach, lean):
    sequence = jax.random.permutation(own_key, number_of)
    heavy_load, ordinary = shares(number_of, rows * top, reach, lean, True), shares(number_of, rows * top, reach, lean, False)
    places = jnp.arange(number_of)

    def named(lengths, turn):
        used = int((lengths > 0).sum())
        fixed = max(1, used // 4)
        passed = fixed + (places - fixed + turn * (used - fixed)) % max(1, number_of - fixed)
        return jnp.zeros((number_of,), jnp.int32).at[sequence[jnp.where(places < fixed, places, passed)]].set(jnp.asarray(lengths, jnp.int32))

    lengths = jnp.where(number % 4 == 0, named(heavy_load, number // 4), named(ordinary, number - number // 4 - 1))
    mixed = jax.random.permutation(jax.random.fold_in(own, 3), number_of)
    donor, taker = mixed[0:number_of // 2 * 2:2], mixed[1:number_of // 2 * 2:2]
    room = jnp.minimum(lengths[donor] - 1, reach - lengths[taker]) // 2
    room = jnp.where((donor == sequence[0]) | (taker == sequence[0]) | (lengths[taker] == 0), 0, jnp.maximum(room, 0))
    passed = jax.random.randint(jax.random.fold_in(own, 4), (number_of // 2,), 0, 1 << 20) % (room + 1)
    lengths = lengths.at[donor].add(-passed).at[taker].add(passed)
    items = jnp.searchsorted(jnp.cumsum(lengths), jnp.arange(rows * top), side="right").astype(jnp.int32)
    table = items.reshape(top, rows).T
    table = table[jax.random.permutation(jax.random.fold_in(own, 1), rows)]
    turn = jax.random.randint(jax.random.fold_in(own, 2), (rows, 1), 0, top)
    return jnp.take_along_axis(table, (jnp.arange(top)[None, :] + turn) % top, axis=1)


def shares(count, total, bound, lean, full):
    portions = [(1 << 20) // math.isqrt(grade ** lean) + 1 for grade in range(1, count + 1)]
    largest = bound if full else min(bound, max(-(-total // count), total * portions[0] // sum(portions)))
    least = 1 if total - largest >= count - 1 else 0
    counts, rest = [largest] + [least] * (count - 1), total - largest - least * (count - 1)
    while rest > 0:
        movable = [i for i in range(1, count) if counts[i] < largest] or [i for i in range(1, count) if counts[i] < bound]
        mass, remaining = sum([portions[i] for i in movable]), rest
        for i in movable:
            extra = min(bound - counts[i], max(1, remaining * portions[i] // mass), rest)
            counts[i] = counts[i] + extra
            rest = rest - extra
    return np.array(counts)


def noise(key, dims, deviation, bound, split=(), kind=jnp.bfloat16):
    result = deviation * jax.random.normal(key, dims, jnp.float32)
    if split:
        result = result * block_scale(key, dims, split, -0.22, 0.18)
    return jnp.clip(result, -bound, bound).astype(kind)


def setup_inputs(seed: int = 0) -> dict:
    streams_of = jax.random.split(jax.random.key(seed), 6)
    queries = draw_queries(jax.random.fold_in(streams_of[5], 71), 0)
    keys = draw_keys(jax.random.fold_in(streams_of[5], 71), 0)
    values = noise(streams_of[2], (TOKENS, KV_HEADS * HEAD_DIM), 1.0, 6.0, ((0, 8), (1, 4)))
    segment_ids = jnp.searchsorted(jnp.cumsum(uneven(streams_of[3], SEGMENTS, TOKENS, MOST_LEN, 2)), jnp.arange(TOKENS), side="right").astype(jnp.int32)
    cache_owner_keys = jax.random.split(jax.random.fold_in(streams_of[4], 1), TOKENS // TOK_GRP)
    cache_owner_turns = jax.random.permutation(jax.random.fold_in(streams_of[4], 3), TOKENS // TOK_GRP)
    cache_owner = jax.vmap(lambda own, number: deal_out(jax.random.fold_in(streams_of[4], 2), own, number, TOK_GRP, N_GRP, 1, CAP, 2))(cache_owner_keys, cache_owner_turns).reshape((TOKENS, 1))
    return dict(queries=queries, keys=keys, values=values, segment_ids=segment_ids, cache_owner=cache_owner)


rope_base = 10000.0


def positions(labels):
    counter = jnp.arange(labels.shape[0], dtype=jnp.int32)
    starts_here = jnp.concatenate([jnp.ones((1,), dtype=jnp.bool_), labels[1:] != labels[:-1]])
    begins = lax.cummax(jnp.where(starts_here, counter, 0), axis=0)
    return counter - begins


def rotate(tensor, places):
    half_dim = tensor.shape[-1] // 2
    inverse = jnp.exp(jnp.arange(half_dim, dtype=jnp.float32) * (-2.0 * math.log(rope_base) / tensor.shape[-1]))
    angles = places.astype(jnp.float32)[:, None] * inverse[None, :]
    cosine = jnp.cos(angles)[:, None, :]
    sine_part = jnp.sin(angles)[:, None, :]
    first_half = tensor[..., :half_dim].astype(jnp.float32)
    second_half = tensor[..., half_dim:].astype(jnp.float32)
    joined = jnp.concatenate([first_half * cosine - second_half * sine_part, second_half * cosine + first_half * sine_part], -1)
    return joined.astype(jnp.bfloat16)


def reference(queries, keys, values, segment_ids, cache_owner):
    block_rows = TOK_GRP
    key_width = KV_HEADS * HEAD_DIM
    group_size = HEADS // KV_HEADS
    scale = HEAD_DIM ** -0.5
    places = positions(segment_ids)
    q_rot = rotate(queries.reshape(TOKENS, HEADS, HEAD_DIM), places)
    k_rot = rotate(keys.reshape(TOKENS, KV_HEADS, HEAD_DIM), places)
    zero_rows = jnp.zeros((block_rows, KV_HEADS, HEAD_DIM), jnp.bfloat16)
    key_padded = jnp.concatenate([zero_rows, k_rot], 0)
    value_padded = jnp.concatenate([zero_rows, values.reshape(TOKENS, KV_HEADS, HEAD_DIM)], 0)
    label_padded = jnp.concatenate([jnp.full((block_rows,), -1, jnp.int32), segment_ids], 0)

    def one_group(group_index):
        begin = (group_index * block_rows).astype(jnp.int32)
        query_block = lax.dynamic_slice_in_dim(q_rot, begin, block_rows, 0)
        query_block = query_block.reshape(block_rows, KV_HEADS, group_size, HEAD_DIM).astype(jnp.float32)
        key_block = lax.dynamic_slice_in_dim(key_padded, begin, 2 * block_rows, 0).astype(jnp.float32)
        value_block = lax.dynamic_slice_in_dim(value_padded, begin, 2 * block_rows, 0).astype(jnp.float32)
        query_labels = lax.dynamic_slice_in_dim(segment_ids, begin, block_rows, 0)
        key_labels = lax.dynamic_slice_in_dim(label_padded, begin, 2 * block_rows, 0)
        row_index = jnp.arange(block_rows, dtype=jnp.int32)[:, None]
        column_index = jnp.arange(2 * block_rows, dtype=jnp.int32)[None, :]
        allowed = (query_labels[:, None] == key_labels[None, :]) & (column_index <= row_index + block_rows)
        scores = jnp.einsum("tkgd,ukd->kgtu", query_block, key_block) * scale
        masked = jnp.where(allowed, scores, -1e30)
        row_max = jnp.max(masked, -1, keepdims=True)
        expo_terms = jnp.where(allowed, jnp.exp(masked - row_max), 0.0)
        weights = (expo_terms / jnp.sum(expo_terms, -1, keepdims=True)).astype(jnp.bfloat16)
        mixed = jnp.einsum("kgtu,ukd->tkgd", weights.astype(jnp.float32), value_block)
        return mixed.reshape(block_rows, HEADS * HEAD_DIM).astype(jnp.bfloat16)

    attention = lax.map(one_group, jnp.arange(N_GRP, dtype=jnp.int32)).reshape(TOKENS, HEADS * HEAD_DIM)

    owners = cache_owner[:, 0].reshape(N_GRP, block_rows)
    one_hot = (owners[:, :, None] == jnp.arange(N_GRP, dtype=jnp.int32)[None, None, :]).astype(jnp.int32)
    ranks = jnp.sum(jnp.cumsum(one_hot, 1) * one_hot, 2) - 1
    sources = jnp.arange(N_GRP, dtype=jnp.int32)[:, None]
    slots = owners * SLOTS + (ranks // QCAP) * (N_GRP * QCAP) + sources * QCAP + ranks % QCAP
    slots = slots.reshape(TOKENS).astype(jnp.int32)
    key_cache = jnp.zeros((N_GRP * SLOTS, key_width), jnp.bfloat16).at[slots].set(k_rot.reshape(TOKENS, key_width))
    value_cache = jnp.zeros((N_GRP * SLOTS, key_width), jnp.bfloat16).at[slots].set(values)
    return attention, key_cache, value_cache
```

```python
import functools
import math

import jax
import jax.numpy as jnp
import ml_dtypes
import numpy as np
from jax import lax
from jax.experimental import pallas as pl
from jax.experimental.pallas import tpu as pltpu
from jax.sharding import PartitionSpec as P

HEAD_DIM = 128
REACH = 256
TILE = 128
MESH = pl.DeviceIdType.MESH
PASS_AT = 0
THEIRS_AT = 1


rope_base = 10000.0


def shifted(block, axis, distance):
    devices = range(lax.axis_size(axis))
    route = [(i - distance, i) for i in devices if i - distance in devices]
    return lax.ppermute(block, axis, route)


def earlier_alike(labels):
    alike = labels[:, None] == labels[None, :]
    order = jnp.arange(labels.shape[0], dtype=jnp.int32)
    return jnp.sum((alike & (order[None, :] < order[:, None])).astype(jnp.int32), 1)


def rotate(tensor, places):
    half_dim = tensor.shape[-1] // 2
    inverse = jnp.exp(
        jnp.arange(half_dim, dtype=jnp.float32) * (-2.0 * math.log(rope_base) / tensor.shape[-1])
    )
    angles = places.astype(jnp.float32)[:, None] * inverse[None, :]
    cosine = jnp.cos(angles)[:, None, :]
    sine_part = jnp.sin(angles)[:, None, :]
    first_half = tensor[..., :half_dim].astype(jnp.float32)
    second_half = tensor[..., half_dim:].astype(jnp.float32)
    joined = jnp.concatenate(
        [
            first_half * cosine - second_half * sine_part,
            second_half * cosine + first_half * sine_part,
        ],
        -1,
    )
    return joined.astype(jnp.bfloat16)


def plain_shards(queries, keys, values, segment_ids, cache_owner):
    block_rows = queries.shape[0]
    key_width = keys.shape[1]
    query_heads = queries.shape[1] // HEAD_DIM
    key_heads = key_width // HEAD_DIM
    group_size = query_heads // key_heads
    scale = HEAD_DIM ** (-0.5)
    groups = lax.axis_size("grp")
    tp_count = lax.axis_size("tp")
    group_index = lax.axis_index("grp")
    quarter_cap = max(1, block_rows // (2 * groups))
    own_labels = lax.dynamic_slice_in_dim(segment_ids, group_index * block_rows, block_rows, 0)
    prior_labels = lax.dynamic_slice_in_dim(
        segment_ids, jnp.maximum(group_index - 1, 0) * block_rows, block_rows, 0
    )
    has_prior = group_index > 0
    carried = jnp.where(has_prior, jnp.sum((prior_labels == own_labels[0]).astype(jnp.int32)), 0)
    places = earlier_alike(own_labels) + jnp.where(own_labels == own_labels[0], carried, 0)
    q_rot = rotate(queries.reshape(block_rows, query_heads, HEAD_DIM), places)
    k_rot = rotate(keys.reshape(block_rows, key_heads, HEAD_DIM), places).reshape(
        block_rows, key_width
    )
    prior_keys, prior_values = shifted((k_rot, values), "grp", 1)
    row_index = jnp.arange(block_rows, dtype=jnp.int32)[:, None]
    column_index = jnp.arange(block_rows, dtype=jnp.int32)[None, :]
    local_mask = (own_labels[:, None] == own_labels[None, :]) & (column_index <= row_index)
    prior_mask = (own_labels[:, None] == prior_labels[None, :]) & has_prior

    def head_major(rows_flat):
        return rows_flat.reshape(-1, key_heads, HEAD_DIM).transpose(1, 0, 2)

    local_key_stack = head_major(k_rot)
    local_value_stack = head_major(values)
    prior_key_stack = head_major(prior_keys)
    prior_value_stack = head_major(prior_values)
    joint_mask = jnp.concatenate([prior_mask, local_mask], 1)
    joint_key_stack = jnp.concatenate([prior_key_stack, local_key_stack], 1)
    joint_value_stack = jnp.concatenate([prior_value_stack, local_value_stack], 1)
    query_stack = q_rot.transpose(1, 0, 2)
    head_source = jnp.arange(query_heads, dtype=jnp.int32) // group_size

    def attend(pieces):
        query_rows, source_head = pieces
        key_rows = lax.dynamic_index_in_dim(joint_key_stack, source_head, 0, keepdims=False)
        value_rows = lax.dynamic_index_in_dim(joint_value_stack, source_head, 0, keepdims=False)
        scores = (
            jnp.einsum("td,ud->tu", query_rows, key_rows, preferred_element_type=jnp.float32)
            * scale
        )
        masked = jnp.where(joint_mask, scores, -1e30)
        row_max = jnp.max(masked, -1, keepdims=True)
        expo_terms = jnp.where(joint_mask, jnp.exp(masked - row_max), 0.0)
        weights = (expo_terms / jnp.sum(expo_terms, -1, keepdims=True)).astype(jnp.bfloat16)
        mixed = jnp.dot(weights, value_rows, preferred_element_type=jnp.float32)
        return mixed.astype(jnp.bfloat16)

    head_outputs = lax.map(attend, (query_stack, head_source))
    attention = head_outputs.transpose(1, 0, 2).reshape(block_rows, query_heads * HEAD_DIM)
    owners = cache_owner[:, 0]
    ranks = earlier_alike(owners)
    send_slot = owners * (tp_count * quarter_cap) + ranks
    buffer_rows = groups * tp_count * quarter_cap
    send_keys = jnp.zeros((buffer_rows, key_width), jnp.bfloat16).at[send_slot].set(k_rot)
    send_values = jnp.zeros((buffer_rows, key_width), jnp.bfloat16).at[send_slot].set(values)
    send_keys = send_keys.reshape(groups, tp_count, quarter_cap, key_width)
    send_values = send_values.reshape(groups, tp_count, quarter_cap, key_width)
    middle_keys, middle_values = (
        lax.all_to_all(send_keys, "tp", split_axis=1, concat_axis=3, tiled=True),
        lax.all_to_all(send_values, "tp", split_axis=1, concat_axis=3, tiled=True),
    )
    got_keys, got_values = (
        lax.all_to_all(middle_keys, "grp", split_axis=0, concat_axis=0, tiled=True),
        lax.all_to_all(middle_values, "grp", split_axis=0, concat_axis=0, tiled=True),
    )
    key_cache = got_keys.reshape(groups * quarter_cap, tp_count * key_width)
    value_cache = got_values.reshape(groups * quarter_cap, tp_count * key_width)
    return (attention, key_cache, value_cache)


def rope_table():
    half_dim = HEAD_DIM // 2
    inverse = np.exp(
        np.arange(half_dim, dtype=np.float32) * np.float32(-2.0 * math.log(rope_base) / HEAD_DIM)
    ).astype(np.float32)
    angles = (np.arange(REACH, dtype=np.float32)[:, None] * inverse[None, :]).astype(np.float32)
    cosine = np.cos(angles.astype(np.float64))
    sine = np.sin(angles.astype(np.float64))
    rest = np.concatenate([cosine, cosine, -sine, sine], 1)
    parts = []
    for _ in range(3):
        part = rest.astype(np.float32).astype(ml_dtypes.bfloat16)
        parts.append(part)
        rest = rest - part.astype(np.float64)
    return np.concatenate(parts, 1)


def kernel(
    groups,
    tps,
    cap,
    q_hbm,
    k_hbm,
    v_hbm,
    table_hbm,
    labels_hbm,
    owner_hbm,
    attn_hbm,
    kc_hbm,
    vc_hbm,
    qbuf,
    kraw,
    kbuf,
    vbuf,
    ksend,
    vsend,
    obuf,
    cos_ref,
    sin_ref,
    lab_row,
    lab_col,
    slot_ref,
    table_ref,
    labels_ref,
    owner_ref,
    in_sem,
    out_sem,
    send_sem,
    recv_sem,
    halo_send,
    halo_recv,
    raw_send,
    raw_recv,
    relay_ref,
    relay_send,
    relay_recv,
    ready_sem,
):
    rows, width = kraw.shape
    key_heads = width // HEAD_DIM
    q_heads = qbuf.shape[1] // HEAD_DIM
    rep = q_heads // key_heads
    steps = rows // TILE
    window = REACH + TILE
    half = groups // 2
    g = lax.axis_index("grp")
    p = lax.axis_index("tp")
    side = g // half
    y = lax.rem(g, 2)
    first_layer = g < 2
    last_layer = g >= groups - 2
    outer = first_layer | last_layer
    inner = jnp.logical_not(outer)
    partner = jnp.where(side == 0, jnp.minimum(g + 2, groups - 1), jnp.maximum(g - 2, 0))
    own_start = REACH
    partner_start = REACH + rows

    barrier = pltpu.get_barrier_semaphore()

    @pl.when(inner)
    def _():
        pl.semaphore_signal(barrier, inc=1, device_id=(partner, p), device_id_type=MESH)

    @pl.when(inner & (side == 0))
    def _():
        above = jnp.maximum(g - 2, 0)
        pl.semaphore_signal(barrier, inc=1, device_id=(above, p), device_id_type=MESH)

    arrivals = [
        pltpu.make_async_copy(src, dst, in_sem.at[i])
        for i, (src, dst) in enumerate(
            (
                (owner_hbm, owner_ref),
                (labels_hbm, labels_ref),
                (k_hbm, kraw),
                (table_hbm, table_ref),
                (v_hbm, vbuf.at[pl.ds(own_start, rows)]),
                (q_hbm, qbuf),
            )
        )
    ]
    for arrival in arrivals:
        arrival.start()
    owner_in, labels_in, k_in, table_in, v_in, q_in = arrivals

    def greet(i, carry):
        there = groups - 2 + i // tps
        seat = lax.rem(i, tps)

        @pl.when((there != g) | (seat != p))
        def _():
            pl.semaphore_signal(
                barrier, inc=1, device_id=(there, seat), device_id_type=MESH
            )

        return carry

    lax.fori_loop(0, 2 * tps, greet, 0)

    def raw(i, src, dst):
        return pltpu.make_async_remote_copy(
            src_ref=src,
            dst_ref=dst,
            send_sem=raw_send.at[i],
            recv_sem=raw_recv.at[i],
            device_id=(partner, p),
            device_id_type=MESH,
        )

    low, high = rows - REACH, REACH
    raw_v_high = raw(
        0, v_hbm.at[pl.ds(low, high)], vbuf.at[pl.ds(partner_start + low, high)]
    )
    raw_v_low = raw(1, v_hbm.at[pl.ds(0, low)], vbuf.at[pl.ds(partner_start, low)])
    raw_slots = raw(2, slot_ref.at[0], slot_ref.at[1])
    raw_k_high = raw(
        3, kbuf.at[pl.ds(own_start + low, high)], kbuf.at[pl.ds(partner_start, high)]
    )
    gives_raw = g == half - 1
    passes_raw = g == half + 1

    relays = g == 1
    passes_relay = g == half - 1
    to_relay = [
        pltpu.make_async_remote_copy(
            src_ref=src,
            dst_ref=relay_ref.at[i],
            send_sem=relay_send.at[i],
            recv_sem=relay_recv.at[i],
            device_id=(jnp.minimum(g + 2, groups - 1), p),
            device_id_type=MESH,
        )
        for i, src in enumerate((kbuf.at[pl.ds(rows, REACH)], v_hbm.at[pl.ds(low, high)]))
    ]

    @pl.when(jnp.logical_not(last_layer))
    def _():
        pl.semaphore_wait(barrier, 1)

    @pl.when(inner)
    def _():
        raw_v_high.start()

    @pl.when(relays)
    def _():
        to_relay[1].start()

    @pl.when(last_layer)
    def _():
        pl.semaphore_wait(barrier, groups * tps - 1)
        for layer in range(1, groups // 2):
            below = jnp.maximum(g - 2 * layer, 0)
            pl.semaphore_signal(ready_sem, inc=1, device_id=(below, p), device_id_type=MESH)

    owner_in.wait()
    owners = owner_ref[...]
    owner_pad = -(-groups // 16) * 16
    one_hot = (lax.broadcasted_iota(jnp.int32, (owner_pad, rows), 0) == owners).astype(jnp.float32)
    earlier = (
        lax.broadcasted_iota(jnp.int32, (rows, rows), 0)
        < lax.broadcasted_iota(jnp.int32, (rows, rows), 1)
    ).astype(jnp.float32)
    counts = jnp.dot(
        one_hot.astype(jnp.bfloat16),
        earlier.astype(jnp.bfloat16),
        preferred_element_type=jnp.float32,
    )
    ranks = jnp.sum(counts * one_hot, 0, keepdims=True)
    slot_ref[0] = owners * (tps * cap) + ranks.astype(jnp.int32)

    @pl.when(inner)
    def _():
        raw_slots.start()

    def allowed(b):
        start = pl.multiple_of(b * TILE, TILE)
        line = lab_row[:, pl.ds(start, window)]
        col = lab_col[pl.ds(start, TILE), :]
        col = jnp.concatenate([col] * (window // TILE), 1)
        causal = (
            lax.broadcasted_iota(jnp.int32, (TILE, window), 1)
            <= lax.broadcasted_iota(jnp.int32, (TILE, window), 0) + REACH
        )
        return (col == line) & causal

    def turn(x, cosine, sine):
        return (x * cosine + pltpu.roll(x, HEAD_DIM // 2, 1) * sine).astype(jnp.bfloat16)

    labels_in.wait()
    k_in.wait()
    table_in.wait()
    before = pl.multiple_of(jnp.maximum(g * rows - REACH, 0), 128)
    prior = labels_ref[:, pl.ds(before, REACH)].astype(jnp.float32)
    own = labels_ref[:, pl.ds(pl.multiple_of(g * rows, 128), rows)].astype(jnp.float32)
    lab_row[:, :REACH] = jnp.where(jnp.full(prior.shape, g) > 0, prior, -1.0)
    lab_row[:, REACH:] = own
    for b in range(steps):
        line = own[:, b * TILE : (b + 1) * TILE]
        lab_col[pl.ds(b * TILE, TILE), :] = jnp.transpose(jnp.broadcast_to(line, (TILE, TILE)))

    def rotate_keys(b, carry):
        start = pl.multiple_of(b * TILE, TILE)
        place = jnp.sum(allowed(b).astype(jnp.float32), 1, keepdims=True) - 1.0
        pick = lax.broadcasted_iota(jnp.int32, (TILE, REACH), 1) == place.astype(jnp.int32)
        pick = pick.astype(jnp.float32).astype(jnp.bfloat16)
        found = jnp.dot(pick, table_ref[...], preferred_element_type=jnp.float32)
        wide = 2 * HEAD_DIM
        found = found[:, :wide] + found[:, wide : 2 * wide] + found[:, 2 * wide :]
        cosine, sine = found[:, :HEAD_DIM], found[:, HEAD_DIM:]
        cos_ref[pl.ds(start, TILE), :] = cosine
        sin_ref[pl.ds(start, TILE), :] = sine
        for h in range(key_heads):
            cols = slice(h * HEAD_DIM, (h + 1) * HEAD_DIM)
            x = kraw[pl.ds(start, TILE), cols].astype(jnp.float32)
            kbuf[pl.ds(pl.multiple_of(own_start + start, TILE), TILE), cols] = turn(x, cosine, sine)
        return carry

    lax.fori_loop(0, steps, rotate_keys, 0)

    @pl.when(gives_raw)
    def _():
        raw_k_high.start()

    @pl.when(inner)
    def _():
        raw_v_low.start()

    @pl.when(relays)
    def _():
        to_relay[0].start()

    v_in.wait()

    @pl.when(jnp.logical_not(last_layer))
    def _():
        pl.semaphore_wait(ready_sem, 1)

    lanes_of = ((kbuf, ksend, kc_hbm), (vbuf, vsend, vc_hbm))
    land_cols = pl.ds(pl.multiple_of(p * width, width), width)

    def deal(unit, i, owner, theirs=False, mine=False):
        buf, send, cache = lanes_of[i]
        source = partner if theirs else g
        first = partner_start if theirs else own_start
        land = cache.at[pl.ds(pl.multiple_of(source * cap, cap), cap), land_cols]
        slots = lax.broadcasted_iota(jnp.int32, (tps * cap, rows), 0) + owner * (tps * cap)
        pick = (slots == slot_ref[int(theirs)]).astype(jnp.float32).astype(jnp.bfloat16)
        got = jnp.dot(pick, buf[pl.ds(first, rows), :], preferred_element_type=jnp.float32)
        send[pl.ds(unit * tps, tps)] = got.astype(jnp.bfloat16).reshape(tps, cap, width)
        for j in range(int(mine), tps):
            quarter = lax.rem(p + j, tps)
            pltpu.make_async_remote_copy(
                src_ref=send.at[unit * tps + quarter],
                dst_ref=land,
                send_sem=send_sem.at[i],
                recv_sem=recv_sem.at[i],
                device_id=(owner, quarter),
                device_id_type=MESH,
            ).start()
        if mine:
            pltpu.make_async_copy(send.at[unit * tps + p], land, recv_sem.at[i]).start()

    def deal_far(i):
        def step(s, carry):
            deal(s, i, (1 - side) * half + s + y * (1 - 2 * lax.rem(s, 2)))
            return carry

        lax.fori_loop(0, half, step, 0)

    def deal_near(i, theirs):
        first = 0 if theirs else half

        def step(s, carry):
            deal(first + s, i, side * half + lax.rem(g + s + 1, half), theirs)
            return carry

        lax.fori_loop(0, half - 1, step, 0)
        deal(first + half - 1, i, g, theirs, True)

    def halo(src, buf, i, to):
        return pltpu.make_async_remote_copy(
            src_ref=src,
            dst_ref=buf.at[pl.ds(0, REACH)],
            send_sem=halo_send.at[i],
            recv_sem=halo_recv.at[i],
            device_id=(to, p),
            device_id_type=MESH,
        )

    following = jnp.minimum(g + 1, groups - 1)
    preceding = jnp.maximum(g - 1, 0)
    gives_halo = (g != 1) & (g != half - 1) & (g < groups - 1)
    bufs = (kbuf, vbuf)
    halos = [halo(buf.at[pl.ds(rows, REACH)], buf, i, following) for i, buf in enumerate(bufs)]
    passed_relay = [halo(relay_ref.at[i], buf, 2 + i, preceding) for i, buf in enumerate(bufs)]
    passed_raw = [
        halo(buf.at[pl.ds(start, REACH)], buf, 2 + i, preceding)
        for i, (buf, start) in enumerate(((kbuf, partner_start), (vbuf, 2 * rows)))
    ]
    gets_passed = (g == 2) | (g == half)

    @pl.when(gives_halo)
    def _():
        for copy in halos:
            copy.start()

    deal_near(1, False)
    deal_near(0, False)
    @pl.when(gives_raw)
    def _():
        raw_k_high.wait_send()

    @pl.when(inner)
    def _():
        raw_v_high.wait_send()
        raw_v_low.wait_send()

    @pl.when(outer)
    def _():
        deal_far(1)

    deal_far(0)

    @pl.when(g == 0)
    def _():
        kbuf[:REACH, :] = jnp.zeros((REACH, width), jnp.bfloat16)
        vbuf[:REACH, :] = jnp.zeros((REACH, width), jnp.bfloat16)

    q_in.wait()

    def pass_relay():
        for copy in to_relay:
            copy.wait_recv()
        for copy in passed_relay:
            copy.start()

    def pass_raw():
        raw_k_high.wait_recv()
        raw_v_high.wait_recv()
        for copy in passed_raw:
            copy.start()

    def deal_their_values():
        @pl.when(jnp.logical_not(passes_raw))
        def _():
            raw_v_high.wait_recv()

        raw_v_low.wait_recv()
        raw_slots.wait_recv()
        deal_near(1, True)

    errands = (
        (PASS_AT, passes_relay, pass_relay),
        (PASS_AT, passes_raw, pass_raw),
        (THEIRS_AT, inner, deal_their_values),
    )

    factor = HEAD_DIM**-0.5 * math.log2(math.e)
    ahead = steps - REACH // TILE

    def attend(it, carry):
        b = lax.rem(it + REACH // TILE, steps)
        start = pl.multiple_of(b * TILE, TILE)

        for turn_at, whose, action in errands:
            if turn_at < steps:
                pl.when((it == turn_at) & whose)(action)

        @pl.when((it == ahead) & (g > 0) & jnp.logical_not(gets_passed))
        def _():
            for copy in halos:
                copy.wait_recv()

        @pl.when((it == ahead) & gets_passed)
        def _():
            for copy in passed_raw:
                copy.wait_recv()

        mask = allowed(b)
        cosine = cos_ref[pl.ds(start, TILE), :]
        sine = sin_ref[pl.ds(start, TILE), :]
        for h in range(key_heads):
            cols = slice(h * HEAD_DIM, (h + 1) * HEAD_DIM)
            keys = kbuf[pl.ds(start, window), cols]
            vals = vbuf[pl.ds(start, window), cols]
            for r in range(rep):
                lanes = slice((h * rep + r) * HEAD_DIM, (h * rep + r + 1) * HEAD_DIM)
                q = turn(qbuf[pl.ds(start, TILE), lanes].astype(jnp.float32), cosine, sine)
                scores = lax.dot_general(
                    q, keys, (((1,), (1,)), ((), ())), preferred_element_type=jnp.float32
                )
                scores = jnp.where(mask, scores * factor, -1e30)
                expo = jnp.exp2(scores - jnp.max(scores, -1, keepdims=True))
                total = jnp.sum(expo, -1, keepdims=True)
                mixed = jnp.dot(
                    expo.astype(jnp.bfloat16), vals, preferred_element_type=jnp.float32
                )
                obuf[pl.ds(start, TILE), lanes] = (mixed / total).astype(jnp.bfloat16)
        return carry

    lax.fori_loop(0, steps, attend, 0)
    out = pltpu.make_async_copy(obuf, attn_hbm, out_sem)
    out.start()

    for turn_at, whose, action in errands:
        if turn_at >= steps:
            pl.when(whose)(action)

    @pl.when(inner)
    def _():
        raw_slots.wait_send()

    @pl.when(gives_halo)
    def _():
        for copy in halos:
            copy.wait_send()

    @pl.when(relays)
    def _():
        for copy in to_relay:
            copy.wait_send()

    @pl.when(passes_relay)
    def _():
        for copy in passed_relay:
            copy.wait_send()

    @pl.when(passes_raw)
    def _():
        for copy in passed_raw:
            copy.wait_send()

    blocks = groups * tps
    for i, (_, send, cache) in enumerate(lanes_of):

        def wait_sent(fewer):
            sent = send.at[pl.ds(0, blocks - fewer)]
            pltpu.make_async_copy(sent, sent, send_sem.at[i]).wait()

        if i == 0:
            wait_sent(1)
        else:
            pl.when(outer)(functools.partial(wait_sent, 1))
            pl.when(inner)(functools.partial(wait_sent, 2))
        pltpu.make_async_copy(cache, cache, recv_sem.at[i]).wait()
    out.wait()


def hand_over(*arrays):
    count, pieces = len(arrays), 4

    def copy_kernel(*refs):
        sem = refs[-1]
        copies = []
        for i in range(count):
            piece = arrays[i].shape[0] // pieces
            for j in range(pieces):
                part = pl.ds(j * piece, piece)
                copies.append(
                    pltpu.make_async_copy(
                        refs[i].at[part], refs[count + i].at[part], sem.at[i, j]
                    )
                )
        for copy in copies:
            copy.start()
        for copy in copies:
            copy.wait()

    anywhere = pl.BlockSpec(memory_space=pl.ANY)
    return pl.pallas_call(
        copy_kernel,
        out_shape=tuple(jax.ShapeDtypeStruct(a.shape, a.dtype) for a in arrays),
        in_specs=[anywhere] * count,
        out_specs=(anywhere,) * count,
        scratch_shapes=[pltpu.SemaphoreType.DMA((count, pieces))],
        compiler_params=pltpu.CompilerParams(vmem_limit_bytes=16 * 2**20),
    )(*arrays)


def shards(queries, keys, values, segment_ids, cache_owner):
    rows, width = keys.shape
    groups = lax.axis_size("grp")
    tps = lax.axis_size("tp")
    cap = max(1, rows // (2 * groups))
    if cap % 16 or rows % TILE or rows < 2 * REACH or groups != 8:
        return plain_shards(queries, keys, values, segment_ids, cache_owner)
    anywhere = pl.BlockSpec(memory_space=pl.ANY)
    hbm = pl.BlockSpec(memory_space=pltpu.HBM)
    bf16 = jnp.bfloat16
    table = jnp.asarray(rope_table())
    cache = jax.ShapeDtypeStruct((groups * cap, tps * width), bf16)
    landed = pl.pallas_call(
        functools.partial(kernel, groups, tps, cap),
        out_shape=(jax.ShapeDtypeStruct(queries.shape, bf16), cache, cache),
        in_specs=[hbm] * 6,
        out_specs=(anywhere, anywhere, anywhere),
        scratch_shapes=[
            pltpu.VMEM(queries.shape, bf16),
            pltpu.VMEM((rows, width), bf16),
            pltpu.VMEM((REACH + rows + REACH, width), bf16),
            pltpu.VMEM((REACH + 2 * rows, width), bf16),
            pltpu.VMEM((groups * tps, cap, width), bf16),
            pltpu.VMEM((groups * tps, cap, width), bf16),
            pltpu.VMEM(queries.shape, bf16),
            pltpu.VMEM((rows, HEAD_DIM), jnp.float32),
            pltpu.VMEM((rows, HEAD_DIM), jnp.float32),
            pltpu.VMEM((1, REACH + rows), jnp.float32),
            pltpu.VMEM((rows, TILE), jnp.float32),
            pltpu.VMEM((2, 1, rows), jnp.int32),
            pltpu.VMEM(table.shape, bf16),
            pltpu.VMEM((1, segment_ids.shape[0]), jnp.int32),
            pltpu.VMEM((1, rows), jnp.int32),
            pltpu.SemaphoreType.DMA((6,)),
            pltpu.SemaphoreType.DMA,
            pltpu.SemaphoreType.DMA((2,)),
            pltpu.SemaphoreType.DMA((2,)),
            pltpu.SemaphoreType.DMA((4,)),
            pltpu.SemaphoreType.DMA((4,)),
            pltpu.SemaphoreType.DMA((4,)),
            pltpu.SemaphoreType.DMA((4,)),
            pltpu.VMEM((2, REACH, width), bf16),
            pltpu.SemaphoreType.DMA((2,)),
            pltpu.SemaphoreType.DMA((2,)),
            pltpu.SemaphoreType.REGULAR,
        ],
        compiler_params=pltpu.CompilerParams(
            collective_id=0, has_side_effects=True, vmem_limit_bytes=40 * 2**20
        ),
    )(
        *(
            pltpu.with_memory_space_constraint(operand, pltpu.HBM)
            for operand in (
                queries,
                keys,
                values,
                table,
                segment_ids.reshape(1, -1),
                cache_owner.reshape(1, -1),
            )
        )
    )
    return hand_over(*landed)


def solution(mesh):
    in_specs = (P("grp", "tp"), P("grp", "tp"), P("grp", "tp"), P(), P("grp", None))
    out_specs = (P("grp", "tp"), P(("grp", "tp"), None), P(("grp", "tp"), None))
    return jax.shard_map(shards, mesh=mesh, in_specs=in_specs, out_specs=out_specs, check_vma=False)
```

```python
import functools
import math

import jax
import jax.numpy as jnp
import ml_dtypes
import numpy as np
from jax import lax
from jax.experimental import pallas as pl
from jax.experimental.pallas import tpu as pltpu
from jax.sharding import PartitionSpec as P

HEAD_DIM = 128
REACH = 256
TILE = 128
MESH = pl.DeviceIdType.MESH
PASS_AT = 0
LATE_AT = 1
GIVE_AT = 1
THEIRS_AT = 1
KEYS_AT = 3


rope_base = 10000.0


def shifted(block, axis, distance):
    devices = range(lax.axis_size(axis))
    route = [(i - distance, i) for i in devices if i - distance in devices]
    return lax.ppermute(block, axis, route)


def earlier_alike(labels):
    alike = labels[:, None] == labels[None, :]
    order = jnp.arange(labels.shape[0], dtype=jnp.int32)
    return jnp.sum((alike & (order[None, :] < order[:, None])).astype(jnp.int32), 1)


def rotate(tensor, places):
    half_dim = tensor.shape[-1] // 2
    inverse = jnp.exp(
        jnp.arange(half_dim, dtype=jnp.float32) * (-2.0 * math.log(rope_base) / tensor.shape[-1])
    )
    angles = places.astype(jnp.float32)[:, None] * inverse[None, :]
    cosine = jnp.cos(angles)[:, None, :]
    sine_part = jnp.sin(angles)[:, None, :]
    first_half = tensor[..., :half_dim].astype(jnp.float32)
    second_half = tensor[..., half_dim:].astype(jnp.float32)
    joined = jnp.concatenate(
        [
            first_half * cosine - second_half * sine_part,
            second_half * cosine + first_half * sine_part,
        ],
        -1,
    )
    return joined.astype(jnp.bfloat16)


def plain_shards(queries, keys, values, segment_ids, cache_owner):
    block_rows = queries.shape[0]
    key_width = keys.shape[1]
    query_heads = queries.shape[1] // HEAD_DIM
    key_heads = key_width // HEAD_DIM
    group_size = query_heads // key_heads
    scale = HEAD_DIM ** (-0.5)
    groups = lax.axis_size("grp")
    tp_count = lax.axis_size("tp")
    group_index = lax.axis_index("grp")
    quarter_cap = max(1, block_rows // (2 * groups))
    own_labels = lax.dynamic_slice_in_dim(segment_ids, group_index * block_rows, block_rows, 0)
    prior_labels = lax.dynamic_slice_in_dim(
        segment_ids, jnp.maximum(group_index - 1, 0) * block_rows, block_rows, 0
    )
    has_prior = group_index > 0
    carried = jnp.where(has_prior, jnp.sum((prior_labels == own_labels[0]).astype(jnp.int32)), 0)
    places = earlier_alike(own_labels) + jnp.where(own_labels == own_labels[0], carried, 0)
    q_rot = rotate(queries.reshape(block_rows, query_heads, HEAD_DIM), places)
    k_rot = rotate(keys.reshape(block_rows, key_heads, HEAD_DIM), places).reshape(
        block_rows, key_width
    )
    prior_keys, prior_values = shifted((k_rot, values), "grp", 1)
    row_index = jnp.arange(block_rows, dtype=jnp.int32)[:, None]
    column_index = jnp.arange(block_rows, dtype=jnp.int32)[None, :]
    local_mask = (own_labels[:, None] == own_labels[None, :]) & (column_index <= row_index)
    prior_mask = (own_labels[:, None] == prior_labels[None, :]) & has_prior

    def head_major(rows_flat):
        return rows_flat.reshape(-1, key_heads, HEAD_DIM).transpose(1, 0, 2)

    local_key_stack = head_major(k_rot)
    local_value_stack = head_major(values)
    prior_key_stack = head_major(prior_keys)
    prior_value_stack = head_major(prior_values)
    joint_mask = jnp.concatenate([prior_mask, local_mask], 1)
    joint_key_stack = jnp.concatenate([prior_key_stack, local_key_stack], 1)
    joint_value_stack = jnp.concatenate([prior_value_stack, local_value_stack], 1)
    query_stack = q_rot.transpose(1, 0, 2)
    head_source = jnp.arange(query_heads, dtype=jnp.int32) // group_size

    def attend(pieces):
        query_rows, source_head = pieces
        key_rows = lax.dynamic_index_in_dim(joint_key_stack, source_head, 0, keepdims=False)
        value_rows = lax.dynamic_index_in_dim(joint_value_stack, source_head, 0, keepdims=False)
        scores = (
            jnp.einsum("td,ud->tu", query_rows, key_rows, preferred_element_type=jnp.float32)
            * scale
        )
        masked = jnp.where(joint_mask, scores, -1e30)
        row_max = jnp.max(masked, -1, keepdims=True)
        expo_terms = jnp.where(joint_mask, jnp.exp(masked - row_max), 0.0)
        weights = (expo_terms / jnp.sum(expo_terms, -1, keepdims=True)).astype(jnp.bfloat16)
        mixed = jnp.dot(weights, value_rows, preferred_element_type=jnp.float32)
        return mixed.astype(jnp.bfloat16)

    head_outputs = lax.map(attend, (query_stack, head_source))
    attention = head_outputs.transpose(1, 0, 2).reshape(block_rows, query_heads * HEAD_DIM)
    owners = cache_owner[:, 0]
    ranks = earlier_alike(owners)
    send_slot = owners * (tp_count * quarter_cap) + ranks
    buffer_rows = groups * tp_count * quarter_cap
    send_keys = jnp.zeros((buffer_rows, key_width), jnp.bfloat16).at[send_slot].set(k_rot)
    send_values = jnp.zeros((buffer_rows, key_width), jnp.bfloat16).at[send_slot].set(values)
    send_keys = send_keys.reshape(groups, tp_count, quarter_cap, key_width)
    send_values = send_values.reshape(groups, tp_count, quarter_cap, key_width)
    middle_keys, middle_values = (
        lax.all_to_all(send_keys, "tp", split_axis=1, concat_axis=3, tiled=True),
        lax.all_to_all(send_values, "tp", split_axis=1, concat_axis=3, tiled=True),
    )
    got_keys, got_values = (
        lax.all_to_all(middle_keys, "grp", split_axis=0, concat_axis=0, tiled=True),
        lax.all_to_all(middle_values, "grp", split_axis=0, concat_axis=0, tiled=True),
    )
    key_cache = got_keys.reshape(groups * quarter_cap, tp_count * key_width)
    value_cache = got_values.reshape(groups * quarter_cap, tp_count * key_width)
    return (attention, key_cache, value_cache)


def rope_table():
    half_dim = HEAD_DIM // 2
    inverse = np.exp(
        np.arange(half_dim, dtype=np.float32) * np.float32(-2.0 * math.log(rope_base) / HEAD_DIM)
    ).astype(np.float32)
    angles = (np.arange(REACH, dtype=np.float32)[:, None] * inverse[None, :]).astype(np.float32)
    cosine = np.cos(angles.astype(np.float64))
    sine = np.sin(angles.astype(np.float64))
    rest = np.concatenate([cosine, cosine, -sine, sine], 1)
    parts = []
    for _ in range(3):
        part = rest.astype(np.float32).astype(ml_dtypes.bfloat16)
        parts.append(part)
        rest = rest - part.astype(np.float64)
    return np.concatenate(parts, 1)


def kernel(
    groups,
    tps,
    cap,
    q_hbm,
    k_hbm,
    v_hbm,
    table_hbm,
    labels_hbm,
    owner_hbm,
    attn_hbm,
    kc_hbm,
    vc_hbm,
    qbuf,
    kraw,
    kbuf,
    vbuf,
    ksend,
    vsend,
    obuf,
    cos_ref,
    sin_ref,
    lab_row,
    lab_col,
    slot_ref,
    table_ref,
    labels_ref,
    owner_ref,
    in_sem,
    out_sem,
    send_sem,
    recv_sem,
    halo_send,
    halo_recv,
    raw_send,
    raw_recv,
    relay_ref,
    relay_send,
    relay_recv,
    ready_sem,
    turn_sem,
):
    rows, width = kraw.shape
    key_heads = width // HEAD_DIM
    q_heads = qbuf.shape[1] // HEAD_DIM
    rep = q_heads // key_heads
    steps = rows // TILE
    window = REACH + TILE
    half = groups // 2
    g = lax.axis_index("grp")
    p = lax.axis_index("tp")
    side = g // half
    y = lax.rem(g, 2)
    first_layer = g < 2
    last_layer = g >= groups - 2
    outer = first_layer | last_layer
    inner = jnp.logical_not(outer)
    partner = jnp.where(side == 0, jnp.minimum(g + 2, groups - 1), jnp.maximum(g - 2, 0))
    own_start = REACH
    partner_start = REACH + rows

    barrier = pltpu.get_barrier_semaphore()

    @pl.when(inner)
    def _():
        pl.semaphore_signal(barrier, inc=1, device_id=(partner, p), device_id_type=MESH)

    @pl.when(inner & (side == 0))
    def _():
        above = jnp.maximum(g - 2, 0)
        pl.semaphore_signal(barrier, inc=1, device_id=(above, p), device_id_type=MESH)

    arrivals = [
        pltpu.make_async_copy(src, dst, in_sem.at[i])
        for i, (src, dst) in enumerate(
            (
                (owner_hbm, owner_ref),
                (labels_hbm, labels_ref),
                (k_hbm, kraw),
                (table_hbm, table_ref),
                (v_hbm, vbuf.at[pl.ds(own_start, rows)]),
                (q_hbm, qbuf),
            )
        )
    ]
    for arrival in arrivals:
        arrival.start()
    owner_in, labels_in, k_in, table_in, v_in, q_in = arrivals

    def greet(i, carry):
        there = groups - 2 + i // tps
        seat = lax.rem(i, tps)

        @pl.when((there != g) | (seat != p))
        def _():
            pl.semaphore_signal(
                barrier, inc=1, device_id=(there, seat), device_id_type=MESH
            )

        return carry

    lax.fori_loop(0, 2 * tps, greet, 0)

    def raw(i, src, dst):
        return pltpu.make_async_remote_copy(
            src_ref=src,
            dst_ref=dst,
            send_sem=raw_send.at[i],
            recv_sem=raw_recv.at[i],
            device_id=(partner, p),
            device_id_type=MESH,
        )

    low, high = rows - REACH, REACH
    raw_v_high = raw(
        0, v_hbm.at[pl.ds(low, high)], vbuf.at[pl.ds(partner_start + low, high)]
    )
    raw_v_low = raw(1, v_hbm.at[pl.ds(0, low)], vbuf.at[pl.ds(partner_start, low)])
    raw_slots = raw(2, slot_ref.at[0], slot_ref.at[1])
    raw_k_high = raw(
        3, kbuf.at[pl.ds(own_start + low, high)], kbuf.at[pl.ds(partner_start + low, high)]
    )
    raw_k_low = raw(4, kbuf.at[pl.ds(own_start, low)], kbuf.at[pl.ds(partner_start, low)])
    gives_raw = g == half - 1
    passes_raw = g == half + 1

    relays = g == 1
    passes_relay = g == half - 1
    to_relay = [
        pltpu.make_async_remote_copy(
            src_ref=src,
            dst_ref=relay_ref.at[i],
            send_sem=relay_send.at[i],
            recv_sem=relay_recv.at[i],
            device_id=(jnp.minimum(g + 2, groups - 1), p),
            device_id_type=MESH,
        )
        for i, src in enumerate((kbuf.at[pl.ds(rows, REACH)], v_hbm.at[pl.ds(low, high)]))
    ]

    @pl.when(jnp.logical_not(last_layer))
    def _():
        pl.semaphore_wait(barrier, 1)

    @pl.when(inner)
    def _():
        raw_v_high.start()

    @pl.when(relays)
    def _():
        to_relay[1].start()

    @pl.when(last_layer)
    def _():
        pl.semaphore_wait(barrier, groups * tps - 1)
        for layer in range(1, groups // 2):
            below = jnp.maximum(g - 2 * layer, 0)
            pl.semaphore_signal(ready_sem, inc=1, device_id=(below, p), device_id_type=MESH)

    owner_in.wait()
    owners = owner_ref[...]
    owner_pad = -(-groups // 16) * 16
    one_hot = (lax.broadcasted_iota(jnp.int32, (owner_pad, rows), 0) == owners).astype(jnp.float32)
    earlier = (
        lax.broadcasted_iota(jnp.int32, (rows, rows), 0)
        < lax.broadcasted_iota(jnp.int32, (rows, rows), 1)
    ).astype(jnp.float32)
    counts = jnp.dot(
        one_hot.astype(jnp.bfloat16),
        earlier.astype(jnp.bfloat16),
        preferred_element_type=jnp.float32,
    )
    ranks = jnp.sum(counts * one_hot, 0, keepdims=True)
    slot_ref[0] = owners * (tps * cap) + ranks.astype(jnp.int32)

    @pl.when(inner)
    def _():
        raw_slots.start()

    def allowed(b):
        start = pl.multiple_of(b * TILE, TILE)
        line = lab_row[:, pl.ds(start, window)]
        col = lab_col[pl.ds(start, TILE), :]
        col = jnp.concatenate([col] * (window // TILE), 1)
        causal = (
            lax.broadcasted_iota(jnp.int32, (TILE, window), 1)
            <= lax.broadcasted_iota(jnp.int32, (TILE, window), 0) + REACH
        )
        return (col == line) & causal

    def turn(x, cosine, sine):
        return (x * cosine + pltpu.roll(x, HEAD_DIM // 2, 1) * sine).astype(jnp.bfloat16)

    labels_in.wait()
    k_in.wait()
    table_in.wait()
    before = pl.multiple_of(jnp.maximum(g * rows - REACH, 0), 128)
    prior = labels_ref[:, pl.ds(before, REACH)].astype(jnp.float32)
    own = labels_ref[:, pl.ds(pl.multiple_of(g * rows, 128), rows)].astype(jnp.float32)
    lab_row[:, :REACH] = jnp.where(jnp.full(prior.shape, g) > 0, prior, -1.0)
    lab_row[:, REACH:] = own
    for b in range(steps):
        line = own[:, b * TILE : (b + 1) * TILE]
        lab_col[pl.ds(b * TILE, TILE), :] = jnp.transpose(jnp.broadcast_to(line, (TILE, TILE)))

    def rotate_keys(b, carry):
        start = pl.multiple_of(b * TILE, TILE)
        place = jnp.sum(allowed(b).astype(jnp.float32), 1, keepdims=True) - 1.0
        pick = lax.broadcasted_iota(jnp.int32, (TILE, REACH), 1) == place.astype(jnp.int32)
        pick = pick.astype(jnp.float32).astype(jnp.bfloat16)
        found = jnp.dot(pick, table_ref[...], preferred_element_type=jnp.float32)
        wide = 2 * HEAD_DIM
        found = found[:, :wide] + found[:, wide : 2 * wide] + found[:, 2 * wide :]
        cosine, sine = found[:, :HEAD_DIM], found[:, HEAD_DIM:]
        cos_ref[pl.ds(start, TILE), :] = cosine
        sin_ref[pl.ds(start, TILE), :] = sine
        for h in range(key_heads):
            cols = slice(h * HEAD_DIM, (h + 1) * HEAD_DIM)
            x = kraw[pl.ds(start, TILE), cols].astype(jnp.float32)
            kbuf[pl.ds(pl.multiple_of(own_start + start, TILE), TILE), cols] = turn(x, cosine, sine)
        return carry

    lax.fori_loop(0, steps, rotate_keys, 0)

    @pl.when(gives_raw)
    def _():
        raw_k_high.start()

    @pl.when(inner)
    def _():
        raw_v_low.start()

    @pl.when(gives_raw)
    def _():
        raw_k_low.start()

    @pl.when(relays)
    def _():
        to_relay[0].start()

    v_in.wait()

    @pl.when(jnp.logical_not(last_layer))
    def _():
        pl.semaphore_wait(ready_sem, 1)

    lanes_of = ((kbuf, ksend, kc_hbm), (vbuf, vsend, vc_hbm))
    land_cols = pl.ds(pl.multiple_of(p * width, width), width)

    def deal(unit, i, owner, theirs=False, mine=False):
        buf, send, cache = lanes_of[i]
        source = partner if theirs else g
        first = partner_start if theirs else own_start
        land = cache.at[pl.ds(pl.multiple_of(source * cap, cap), cap), land_cols]
        slots = lax.broadcasted_iota(jnp.int32, (tps * cap, rows), 0) + owner * (tps * cap)
        pick = (slots == slot_ref[int(theirs)]).astype(jnp.float32).astype(jnp.bfloat16)
        got = jnp.dot(pick, buf[pl.ds(first, rows), :], preferred_element_type=jnp.float32)
        send[pl.ds(unit * tps, tps)] = got.astype(jnp.bfloat16).reshape(tps, cap, width)
        for j in range(int(mine), tps):
            quarter = lax.rem(p + j, tps)
            pltpu.make_async_remote_copy(
                src_ref=send.at[unit * tps + quarter],
                dst_ref=land,
                send_sem=send_sem.at[i],
                recv_sem=recv_sem.at[i],
                device_id=(owner, quarter),
                device_id_type=MESH,
            ).start()
        if mine:
            pltpu.make_async_copy(send.at[unit * tps + p], land, recv_sem.at[i]).start()

    def deal_far(i):
        def step(s, carry):
            deal(s, i, (1 - side) * half + s + y * (1 - 2 * lax.rem(s, 2)))
            return carry

        lax.fori_loop(0, half, step, 0)

    def deal_near(i, theirs):
        first = half if not theirs else groups if i == 0 else 0

        def step(s, carry):
            deal(first + s, i, side * half + lax.rem(g + s + 1, half), theirs)
            return carry

        lax.fori_loop(0, half - 1, step, 0)
        deal(first + half - 1, i, g, theirs, True)

    def halo(src, buf, i, to):
        return pltpu.make_async_remote_copy(
            src_ref=src,
            dst_ref=buf.at[pl.ds(0, REACH)],
            send_sem=halo_send.at[i],
            recv_sem=halo_recv.at[i],
            device_id=(to, p),
            device_id_type=MESH,
        )

    following = jnp.minimum(g + 1, groups - 1)
    preceding = jnp.maximum(g - 1, 0)
    gives_halo = (g != 1) & (g != half - 1) & (g < groups - 1)
    bufs = (kbuf, vbuf)
    halos = [halo(buf.at[pl.ds(rows, REACH)], buf, i, following) for i, buf in enumerate(bufs)]
    passed_relay = [halo(relay_ref.at[i], buf, 2 + i, preceding) for i, buf in enumerate(bufs)]
    passed_raw = [
        halo(buf.at[pl.ds(2 * rows, REACH)], buf, 2 + i, preceding)
        for i, buf in enumerate(bufs)
    ]
    gets_passed = (g == 2) | (g == half)
    gives_values = gives_halo & (g != half + 1)
    passes_across = g == half
    gets_across = g == half + 2
    to_across = pltpu.make_async_remote_copy(
        src_ref=vbuf.at[pl.ds(rows, REACH)],
        dst_ref=relay_ref.at[1],
        send_sem=relay_send.at[1],
        recv_sem=relay_recv.at[1],
        device_id=(preceding, p),
        device_id_type=MESH,
    )
    passed_across = halo(relay_ref.at[1], vbuf, 4, jnp.minimum(g + 2, groups - 1))

    @pl.when(gives_halo)
    def _():
        halos[0].start()

    @pl.when(gives_values)
    def _():
        halos[1].start()

    @pl.when(passes_raw)
    def _():
        to_across.start()

    deal_near(1, False)
    deal_near(0, False)

    @pl.when(inner & jnp.logical_not(gives_raw))
    def _():
        raw_v_high.wait_send()
        raw_v_low.wait_send()

    late_far = g == 1

    @pl.when(outer & jnp.logical_not(late_far))
    def _():
        deal_far(1)

    @pl.when(jnp.logical_not(gives_raw | late_far))
    def _():
        deal_far(0)

    @pl.when(g == 0)
    def _():
        kbuf[:REACH, :] = jnp.zeros((REACH, width), jnp.bfloat16)
        vbuf[:REACH, :] = jnp.zeros((REACH, width), jnp.bfloat16)

    q_in.wait()

    def pass_relay():
        for copy in to_relay:
            copy.wait_recv()
        for copy in passed_relay:
            copy.start()

    def pass_across():
        to_across.wait_recv()
        passed_across.start()

    def pass_raw():
        raw_k_high.wait_recv()
        raw_v_high.wait_recv()
        for copy in passed_raw:
            copy.start()

    def deal_their_values():
        @pl.when(jnp.logical_not(passes_raw))
        def _():
            raw_v_high.wait_recv()

        raw_v_low.wait_recv()
        raw_slots.wait_recv()
        deal_near(1, True)

    def deal_their_keys():
        raw_k_low.wait_recv()
        deal_near(0, True)

    def give_turn():
        raw_v_high.wait_send()
        raw_v_low.wait_send()
        raw_k_high.wait_send()
        raw_k_low.wait_send()
        above = jnp.maximum(g - 2, 0)
        pl.semaphore_signal(turn_sem, inc=1, device_id=(above, p), device_id_type=MESH)

    def late_deal():
        pl.semaphore_wait(turn_sem, 1)
        deal_far(1)
        deal_far(0)

    errands = (
        (GIVE_AT, gives_raw, give_turn),
        (LATE_AT, late_far, late_deal),
        (PASS_AT, passes_relay, pass_relay),
        (PASS_AT, passes_raw, pass_raw),
        (PASS_AT, passes_across, pass_across),
        (THEIRS_AT, inner, deal_their_values),
        (KEYS_AT, passes_raw, deal_their_keys),
    )

    factor = HEAD_DIM**-0.5 * math.log2(math.e)
    ahead = steps - REACH // TILE

    def attend(it, carry):
        b = lax.rem(it + REACH // TILE, steps)
        start = pl.multiple_of(b * TILE, TILE)

        for turn_at, whose, action in errands:
            if turn_at < steps:
                pl.when((it == turn_at) & whose)(action)

        @pl.when((it == ahead) & (g > 0) & jnp.logical_not(gets_passed))
        def _():
            halos[0].wait_recv()

        @pl.when((it == ahead) & (g > 0) & jnp.logical_not(gets_passed | gets_across))
        def _():
            halos[1].wait_recv()

        @pl.when((it == ahead) & gets_across)
        def _():
            passed_across.wait_recv()

        @pl.when((it == ahead) & gets_passed)
        def _():
            for copy in passed_raw:
                copy.wait_recv()

        mask = allowed(b)
        cosine = cos_ref[pl.ds(start, TILE), :]
        sine = sin_ref[pl.ds(start, TILE), :]
        for h in range(key_heads):
            cols = slice(h * HEAD_DIM, (h + 1) * HEAD_DIM)
            keys = kbuf[pl.ds(start, window), cols]
            vals = vbuf[pl.ds(start, window), cols]
            for r in range(rep):
                lanes = slice((h * rep + r) * HEAD_DIM, (h * rep + r + 1) * HEAD_DIM)
                q = turn(qbuf[pl.ds(start, TILE), lanes].astype(jnp.float32), cosine, sine)
                scores = lax.dot_general(
                    q, keys, (((1,), (1,)), ((), ())), preferred_element_type=jnp.float32
                )
                scores = jnp.where(mask, scores * factor, -1e30)
                expo = jnp.exp2(scores - jnp.max(scores, -1, keepdims=True))
                total = jnp.sum(expo, -1, keepdims=True)
                mixed = jnp.dot(
                    expo.astype(jnp.bfloat16), vals, preferred_element_type=jnp.float32
                )
                obuf[pl.ds(start, TILE), lanes] = (mixed / total).astype(jnp.bfloat16)
        return carry

    lax.fori_loop(0, steps, attend, 0)
    out = pltpu.make_async_copy(obuf, attn_hbm, out_sem)
    out.start()

    for turn_at, whose, action in errands:
        if turn_at >= steps:
            pl.when(whose)(action)

    @pl.when(inner)
    def _():
        raw_slots.wait_send()

    @pl.when(gives_halo)
    def _():
        halos[0].wait_send()

    @pl.when(gives_values)
    def _():
        halos[1].wait_send()

    @pl.when(passes_across)
    def _():
        passed_across.wait_send()

    @pl.when(relays)
    def _():
        for copy in to_relay:
            copy.wait_send()

    @pl.when(passes_relay)
    def _():
        for copy in passed_relay:
            copy.wait_send()

    @pl.when(passes_raw)
    def _():
        to_across.wait_send()
        for copy in passed_raw:
            copy.wait_send()

    blocks = groups * tps
    for i, (_, send, cache) in enumerate(lanes_of):

        def wait_sent(count):
            sent = send.at[pl.ds(0, count)]
            pltpu.make_async_copy(sent, sent, send_sem.at[i]).wait()

        if i == 0:
            few = half * tps - 1
            pl.when(gives_raw)(functools.partial(wait_sent, few))
            pl.when(passes_raw)(functools.partial(wait_sent, blocks + few - 1))
            plain = jnp.logical_not(gives_raw | passes_raw)
            pl.when(plain)(functools.partial(wait_sent, blocks - 1))
        else:
            pl.when(outer)(functools.partial(wait_sent, blocks - 1))
            pl.when(inner)(functools.partial(wait_sent, blocks - 2))
        pltpu.make_async_copy(cache, cache, recv_sem.at[i]).wait()
    out.wait()


def hand_over(*arrays):
    count, pieces = len(arrays), 4

    def copy_kernel(*refs):
        sem = refs[-1]
        copies = []
        for i in range(count):
            piece = arrays[i].shape[0] // pieces
            for j in range(pieces):
                part = pl.ds(j * piece, piece)
                copies.append(
                    pltpu.make_async_copy(
                        refs[i].at[part], refs[count + i].at[part], sem.at[i, j]
                    )
                )
        for copy in copies:
            copy.start()
        for copy in copies:
            copy.wait()

    anywhere = pl.BlockSpec(memory_space=pl.ANY)
    return pl.pallas_call(
        copy_kernel,
        out_shape=tuple(jax.ShapeDtypeStruct(a.shape, a.dtype) for a in arrays),
        in_specs=[anywhere] * count,
        out_specs=(anywhere,) * count,
        scratch_shapes=[pltpu.SemaphoreType.DMA((count, pieces))],
        compiler_params=pltpu.CompilerParams(vmem_limit_bytes=16 * 2**20),
    )(*arrays)


def shards(queries, keys, values, segment_ids, cache_owner):
    rows, width = keys.shape
    groups = lax.axis_size("grp")
    tps = lax.axis_size("tp")
    cap = max(1, rows // (2 * groups))
    if cap % 16 or rows % TILE or rows < 2 * REACH or groups != 8:
        return plain_shards(queries, keys, values, segment_ids, cache_owner)
    anywhere = pl.BlockSpec(memory_space=pl.ANY)
    hbm = pl.BlockSpec(memory_space=pltpu.HBM)
    bf16 = jnp.bfloat16
    table = jnp.asarray(rope_table())
    cache = jax.ShapeDtypeStruct((groups * cap, tps * width), bf16)
    landed = pl.pallas_call(
        functools.partial(kernel, groups, tps, cap),
        out_shape=(jax.ShapeDtypeStruct(queries.shape, bf16), cache, cache),
        in_specs=[hbm] * 6,
        out_specs=(anywhere, anywhere, anywhere),
        scratch_shapes=[
            pltpu.VMEM(queries.shape, bf16),
            pltpu.VMEM((rows, width), bf16),
            pltpu.VMEM((REACH + 2 * rows, width), bf16),
            pltpu.VMEM((REACH + 2 * rows, width), bf16),
            pltpu.VMEM((groups * tps + groups // 2 * tps, cap, width), bf16),
            pltpu.VMEM((groups * tps, cap, width), bf16),
            pltpu.VMEM(queries.shape, bf16),
            pltpu.VMEM((rows, HEAD_DIM), jnp.float32),
            pltpu.VMEM((rows, HEAD_DIM), jnp.float32),
            pltpu.VMEM((1, REACH + rows), jnp.float32),
            pltpu.VMEM((rows, TILE), jnp.float32),
            pltpu.VMEM((2, 1, rows), jnp.int32),
            pltpu.VMEM(table.shape, bf16),
            pltpu.VMEM((1, segment_ids.shape[0]), jnp.int32),
            pltpu.VMEM((1, rows), jnp.int32),
            pltpu.SemaphoreType.DMA((6,)),
            pltpu.SemaphoreType.DMA,
            pltpu.SemaphoreType.DMA((2,)),
            pltpu.SemaphoreType.DMA((2,)),
            pltpu.SemaphoreType.DMA((5,)),
            pltpu.SemaphoreType.DMA((5,)),
            pltpu.SemaphoreType.DMA((5,)),
            pltpu.SemaphoreType.DMA((5,)),
            pltpu.VMEM((2, REACH, width), bf16),
            pltpu.SemaphoreType.DMA((2,)),
            pltpu.SemaphoreType.DMA((2,)),
            pltpu.SemaphoreType.REGULAR,
            pltpu.SemaphoreType.REGULAR,
        ],
        compiler_params=pltpu.CompilerParams(
            collective_id=0, has_side_effects=True, vmem_limit_bytes=40 * 2**20
        ),
    )(
        *(
            pltpu.with_memory_space_constraint(operand, pltpu.HBM)
            for operand in (
                queries,
                keys,
                values,
                table,
                segment_ids.reshape(1, -1),
                cache_owner.reshape(1, -1),
            )
        )
    )
    return hand_over(*landed)


def solution(mesh):
    in_specs = (P("grp", "tp"), P("grp", "tp"), P("grp", "tp"), P(), P("grp", None))
    out_specs = (P("grp", "tp"), P(("grp", "tp"), None), P(("grp", "tp"), None))
    return jax.shard_map(shards, mesh=mesh, in_specs=in_specs, out_specs=out_specs, check_vma=False)
```

```python
import functools
import math

import jax
import jax.numpy as jnp
import ml_dtypes
import numpy as np
from jax import lax
from jax.experimental import pallas as pl
from jax.experimental.pallas import tpu as pltpu
from jax.sharding import PartitionSpec as P

HEAD_DIM = 128
REACH = 256
TILE = 128
MESH = pl.DeviceIdType.MESH
PASS_AT = 0
LATE_AT = 2
GIVE_AT = 2
THEIRS_AT = 2
KEYS_AT = 4


rope_base = 10000.0


def shifted(block, axis, distance):
    devices = range(lax.axis_size(axis))
    route = [(i - distance, i) for i in devices if i - distance in devices]
    return lax.ppermute(block, axis, route)


def earlier_alike(labels):
    alike = labels[:, None] == labels[None, :]
    order = jnp.arange(labels.shape[0], dtype=jnp.int32)
    return jnp.sum((alike & (order[None, :] < order[:, None])).astype(jnp.int32), 1)


def rotate(tensor, places):
    half_dim = tensor.shape[-1] // 2
    inverse = jnp.exp(
        jnp.arange(half_dim, dtype=jnp.float32) * (-2.0 * math.log(rope_base) / tensor.shape[-1])
    )
    angles = places.astype(jnp.float32)[:, None] * inverse[None, :]
    cosine = jnp.cos(angles)[:, None, :]
    sine_part = jnp.sin(angles)[:, None, :]
    first_half = tensor[..., :half_dim].astype(jnp.float32)
    second_half = tensor[..., half_dim:].astype(jnp.float32)
    joined = jnp.concatenate(
        [
            first_half * cosine - second_half * sine_part,
            second_half * cosine + first_half * sine_part,
        ],
        -1,
    )
    return joined.astype(jnp.bfloat16)


def plain_shards(queries, keys, values, segment_ids, cache_owner):
    block_rows = queries.shape[0]
    key_width = keys.shape[1]
    query_heads = queries.shape[1] // HEAD_DIM
    key_heads = key_width // HEAD_DIM
    group_size = query_heads // key_heads
    scale = HEAD_DIM ** (-0.5)
    groups = lax.axis_size("grp")
    tp_count = lax.axis_size("tp")
    group_index = lax.axis_index("grp")
    quarter_cap = max(1, block_rows // (2 * groups))
    own_labels = lax.dynamic_slice_in_dim(segment_ids, group_index * block_rows, block_rows, 0)
    prior_labels = lax.dynamic_slice_in_dim(
        segment_ids, jnp.maximum(group_index - 1, 0) * block_rows, block_rows, 0
    )
    has_prior = group_index > 0
    carried = jnp.where(has_prior, jnp.sum((prior_labels == own_labels[0]).astype(jnp.int32)), 0)
    places = earlier_alike(own_labels) + jnp.where(own_labels == own_labels[0], carried, 0)
    q_rot = rotate(queries.reshape(block_rows, query_heads, HEAD_DIM), places)
    k_rot = rotate(keys.reshape(block_rows, key_heads, HEAD_DIM), places).reshape(
        block_rows, key_width
    )
    prior_keys, prior_values = shifted((k_rot, values), "grp", 1)
    row_index = jnp.arange(block_rows, dtype=jnp.int32)[:, None]
    column_index = jnp.arange(block_rows, dtype=jnp.int32)[None, :]
    local_mask = (own_labels[:, None] == own_labels[None, :]) & (column_index <= row_index)
    prior_mask = (own_labels[:, None] == prior_labels[None, :]) & has_prior

    def head_major(rows_flat):
        return rows_flat.reshape(-1, key_heads, HEAD_DIM).transpose(1, 0, 2)

    local_key_stack = head_major(k_rot)
    local_value_stack = head_major(values)
    prior_key_stack = head_major(prior_keys)
    prior_value_stack = head_major(prior_values)
    joint_mask = jnp.concatenate([prior_mask, local_mask], 1)
    joint_key_stack = jnp.concatenate([prior_key_stack, local_key_stack], 1)
    joint_value_stack = jnp.concatenate([prior_value_stack, local_value_stack], 1)
    query_stack = q_rot.transpose(1, 0, 2)
    head_source = jnp.arange(query_heads, dtype=jnp.int32) // group_size

    def attend(pieces):
        query_rows, source_head = pieces
        key_rows = lax.dynamic_index_in_dim(joint_key_stack, source_head, 0, keepdims=False)
        value_rows = lax.dynamic_index_in_dim(joint_value_stack, source_head, 0, keepdims=False)
        scores = (
            jnp.einsum("td,ud->tu", query_rows, key_rows, preferred_element_type=jnp.float32)
            * scale
        )
        masked = jnp.where(joint_mask, scores, -1e30)
        row_max = jnp.max(masked, -1, keepdims=True)
        expo_terms = jnp.where(joint_mask, jnp.exp(masked - row_max), 0.0)
        weights = (expo_terms / jnp.sum(expo_terms, -1, keepdims=True)).astype(jnp.bfloat16)
        mixed = jnp.dot(weights, value_rows, preferred_element_type=jnp.float32)
        return mixed.astype(jnp.bfloat16)

    head_outputs = lax.map(attend, (query_stack, head_source))
    attention = head_outputs.transpose(1, 0, 2).reshape(block_rows, query_heads * HEAD_DIM)
    owners = cache_owner[:, 0]
    ranks = earlier_alike(owners)
    send_slot = owners * (tp_count * quarter_cap) + ranks
    buffer_rows = groups * tp_count * quarter_cap
    send_keys = jnp.zeros((buffer_rows, key_width), jnp.bfloat16).at[send_slot].set(k_rot)
    send_values = jnp.zeros((buffer_rows, key_width), jnp.bfloat16).at[send_slot].set(values)
    send_keys = send_keys.reshape(groups, tp_count, quarter_cap, key_width)
    send_values = send_values.reshape(groups, tp_count, quarter_cap, key_width)
    middle_keys, middle_values = (
        lax.all_to_all(send_keys, "tp", split_axis=1, concat_axis=3, tiled=True),
        lax.all_to_all(send_values, "tp", split_axis=1, concat_axis=3, tiled=True),
    )
    got_keys, got_values = (
        lax.all_to_all(middle_keys, "grp", split_axis=0, concat_axis=0, tiled=True),
        lax.all_to_all(middle_values, "grp", split_axis=0, concat_axis=0, tiled=True),
    )
    key_cache = got_keys.reshape(groups * quarter_cap, tp_count * key_width)
    value_cache = got_values.reshape(groups * quarter_cap, tp_count * key_width)
    return (attention, key_cache, value_cache)


def rope_table():
    half_dim = HEAD_DIM // 2
    inverse = np.exp(
        np.arange(half_dim, dtype=np.float32) * np.float32(-2.0 * math.log(rope_base) / HEAD_DIM)
    ).astype(np.float32)
    angles = (np.arange(REACH, dtype=np.float32)[:, None] * inverse[None, :]).astype(np.float32)
    cosine = np.cos(angles.astype(np.float64))
    sine = np.sin(angles.astype(np.float64))
    rest = np.concatenate([cosine, cosine, -sine, sine], 1)
    parts = []
    for _ in range(3):
        part = rest.astype(np.float32).astype(ml_dtypes.bfloat16)
        parts.append(part)
        rest = rest - part.astype(np.float64)
    return np.concatenate(parts, 1)


def kernel(
    groups,
    tps,
    cap,
    q_hbm,
    k_hbm,
    v_hbm,
    table_hbm,
    labels_hbm,
    owner_hbm,
    attn_hbm,
    kc_hbm,
    vc_hbm,
    qbuf,
    kraw,
    kbuf,
    vbuf,
    ksend,
    vsend,
    obuf,
    cos_ref,
    sin_ref,
    lab_row,
    lab_col,
    slot_ref,
    table_ref,
    labels_ref,
    owner_ref,
    in_sem,
    out_sem,
    send_sem,
    recv_sem,
    halo_send,
    halo_recv,
    raw_send,
    raw_recv,
    relay_ref,
    relay_send,
    relay_recv,
    ready_sem,
    turn_sem,
):
    rows, width = kraw.shape
    key_heads = width // HEAD_DIM
    q_heads = qbuf.shape[1] // HEAD_DIM
    rep = q_heads // key_heads
    steps = rows // TILE
    window = REACH + TILE
    half = groups // 2
    g = lax.axis_index("grp")
    p = lax.axis_index("tp")
    side = g // half
    y = lax.rem(g, 2)
    first_layer = g < 2
    last_layer = g >= groups - 2
    outer = first_layer | last_layer
    inner = jnp.logical_not(outer)
    partner = jnp.where(side == 0, jnp.minimum(g + 2, groups - 1), jnp.maximum(g - 2, 0))
    own_start = REACH
    partner_start = REACH + rows

    barrier = pltpu.get_barrier_semaphore()

    @pl.when(inner)
    def _():
        pl.semaphore_signal(barrier, inc=1, device_id=(partner, p), device_id_type=MESH)

    @pl.when(inner & (side == 0))
    def _():
        above = jnp.maximum(g - 2, 0)
        pl.semaphore_signal(barrier, inc=1, device_id=(above, p), device_id_type=MESH)

    arrivals = [
        pltpu.make_async_copy(src, dst, in_sem.at[i])
        for i, (src, dst) in enumerate(
            (
                (owner_hbm, owner_ref),
                (labels_hbm, labels_ref),
                (k_hbm, kraw),
                (table_hbm, table_ref),
                (v_hbm, vbuf.at[pl.ds(own_start, rows)]),
                (q_hbm, qbuf),
            )
        )
    ]
    for arrival in arrivals:
        arrival.start()
    owner_in, labels_in, k_in, table_in, v_in, q_in = arrivals

    def greet(i, carry):
        there = groups - 2 + i // tps
        seat = lax.rem(i, tps)

        @pl.when((there != g) | (seat != p))
        def _():
            pl.semaphore_signal(
                barrier, inc=1, device_id=(there, seat), device_id_type=MESH
            )

        return carry

    lax.fori_loop(0, 2 * tps, greet, 0)

    def raw(i, src, dst):
        return pltpu.make_async_remote_copy(
            src_ref=src,
            dst_ref=dst,
            send_sem=raw_send.at[i],
            recv_sem=raw_recv.at[i],
            device_id=(partner, p),
            device_id_type=MESH,
        )

    low, high = rows - REACH, REACH
    raw_v_high = raw(
        0, v_hbm.at[pl.ds(low, high)], vbuf.at[pl.ds(partner_start + low, high)]
    )
    raw_v_low = raw(1, v_hbm.at[pl.ds(0, low)], vbuf.at[pl.ds(partner_start, low)])
    raw_slots = raw(2, slot_ref.at[0], slot_ref.at[1])
    raw_k_high = raw(
        3, kbuf.at[pl.ds(own_start + low, high)], kbuf.at[pl.ds(partner_start + low, high)]
    )
    raw_k_low = raw(4, kbuf.at[pl.ds(own_start, low)], kbuf.at[pl.ds(partner_start, low)])
    gives_raw = g == half - 1
    passes_raw = g == half + 1

    relays = g == 1
    passes_relay = g == half - 1
    to_relay = [
        pltpu.make_async_remote_copy(
            src_ref=src,
            dst_ref=relay_ref.at[i],
            send_sem=relay_send.at[i],
            recv_sem=relay_recv.at[i],
            device_id=(jnp.minimum(g + 2, groups - 1), p),
            device_id_type=MESH,
        )
        for i, src in enumerate((kbuf.at[pl.ds(rows, REACH)], v_hbm.at[pl.ds(low, high)]))
    ]

    @pl.when(jnp.logical_not(last_layer))
    def _():
        pl.semaphore_wait(barrier, 1)

    @pl.when(inner)
    def _():
        raw_v_high.start()

    @pl.when(relays)
    def _():
        to_relay[1].start()

    @pl.when(last_layer)
    def _():
        pl.semaphore_wait(barrier, groups * tps - 1)
        for layer in range(1, groups // 2):
            below = jnp.maximum(g - 2 * layer, 0)
            pl.semaphore_signal(ready_sem, inc=1, device_id=(below, p), device_id_type=MESH)

    owner_in.wait()
    owners = owner_ref[...]
    owner_pad = -(-groups // 16) * 16
    one_hot = (lax.broadcasted_iota(jnp.int32, (owner_pad, rows), 0) == owners).astype(jnp.float32)
    earlier = (
        lax.broadcasted_iota(jnp.int32, (rows, rows), 0)
        < lax.broadcasted_iota(jnp.int32, (rows, rows), 1)
    ).astype(jnp.float32)
    counts = jnp.dot(
        one_hot.astype(jnp.bfloat16),
        earlier.astype(jnp.bfloat16),
        preferred_element_type=jnp.float32,
    )
    ranks = jnp.sum(counts * one_hot, 0, keepdims=True)
    slot_ref[0] = owners * (tps * cap) + ranks.astype(jnp.int32)

    @pl.when(inner)
    def _():
        raw_slots.start()

    def allowed(b):
        start = pl.multiple_of(b * TILE, TILE)
        line = lab_row[:, pl.ds(start, window)]
        col = lab_col[pl.ds(start, TILE), :]
        col = jnp.concatenate([col] * (window // TILE), 1)
        causal = (
            lax.broadcasted_iota(jnp.int32, (TILE, window), 1)
            <= lax.broadcasted_iota(jnp.int32, (TILE, window), 0) + REACH
        )
        return (col == line) & causal

    def turn(x, cosine, sine):
        return (x * cosine + pltpu.roll(x, HEAD_DIM // 2, 1) * sine).astype(jnp.bfloat16)

    labels_in.wait()
    k_in.wait()
    table_in.wait()
    before = pl.multiple_of(jnp.maximum(g * rows - REACH, 0), 128)
    prior = labels_ref[:, pl.ds(before, REACH)].astype(jnp.float32)
    own = labels_ref[:, pl.ds(pl.multiple_of(g * rows, 128), rows)].astype(jnp.float32)
    lab_row[:, :REACH] = jnp.where(jnp.full(prior.shape, g) > 0, prior, -1.0)
    lab_row[:, REACH:] = own
    for b in range(steps):
        line = own[:, b * TILE : (b + 1) * TILE]
        lab_col[pl.ds(b * TILE, TILE), :] = jnp.transpose(jnp.broadcast_to(line, (TILE, TILE)))

    def rotate_keys(b, carry):
        start = pl.multiple_of(b * TILE, TILE)
        place = jnp.sum(allowed(b).astype(jnp.float32), 1, keepdims=True) - 1.0
        pick = lax.broadcasted_iota(jnp.int32, (TILE, REACH), 1) == place.astype(jnp.int32)
        pick = pick.astype(jnp.float32).astype(jnp.bfloat16)
        found = jnp.dot(pick, table_ref[...], preferred_element_type=jnp.float32)
        wide = 2 * HEAD_DIM
        found = found[:, :wide] + found[:, wide : 2 * wide] + found[:, 2 * wide :]
        cosine, sine = found[:, :HEAD_DIM], found[:, HEAD_DIM:]
        cos_ref[pl.ds(start, TILE), :] = cosine
        sin_ref[pl.ds(start, TILE), :] = sine
        for h in range(key_heads):
            cols = slice(h * HEAD_DIM, (h + 1) * HEAD_DIM)
            x = kraw[pl.ds(start, TILE), cols].astype(jnp.float32)
            kbuf[pl.ds(pl.multiple_of(own_start + start, TILE), TILE), cols] = turn(x, cosine, sine)
        return carry

    lax.fori_loop(0, steps, rotate_keys, 0)

    @pl.when(gives_raw)
    def _():
        raw_k_high.start()

    @pl.when(inner)
    def _():
        raw_v_low.start()

    @pl.when(gives_raw)
    def _():
        raw_k_low.start()

    @pl.when(relays)
    def _():
        to_relay[0].start()

    v_in.wait()

    @pl.when(jnp.logical_not(last_layer))
    def _():
        pl.semaphore_wait(ready_sem, 1)

    lanes_of = ((kbuf, ksend, kc_hbm), (vbuf, vsend, vc_hbm))
    land_cols = pl.ds(pl.multiple_of(p * width, width), width)

    def deal(unit, i, owner, theirs=False, mine=False):
        buf, send, cache = lanes_of[i]
        source = partner if theirs else g
        first = partner_start if theirs else own_start
        land = cache.at[pl.ds(pl.multiple_of(source * cap, cap), cap), land_cols]
        slots = lax.broadcasted_iota(jnp.int32, (tps * cap, rows), 0) + owner * (tps * cap)
        pick = (slots == slot_ref[int(theirs)]).astype(jnp.float32).astype(jnp.bfloat16)
        got = jnp.dot(pick, buf[pl.ds(first, rows), :], preferred_element_type=jnp.float32)
        send[pl.ds(unit * tps, tps)] = got.astype(jnp.bfloat16).reshape(tps, cap, width)
        for j in range(int(mine), tps):
            quarter = lax.rem(p + j, tps) if mine else j
            pltpu.make_async_remote_copy(
                src_ref=send.at[unit * tps + quarter],
                dst_ref=land,
                send_sem=send_sem.at[i],
                recv_sem=recv_sem.at[i],
                device_id=(owner, quarter),
                device_id_type=MESH,
            ).start()
        if mine:
            pltpu.make_async_copy(send.at[unit * tps + p], land, recv_sem.at[i]).start()

    def deal_far(i):
        def step(s, carry):
            turned = jnp.where(side == 0, 2 - 2 * lax.rem(s, 2) + s // 2, 2 * lax.rem(s, 2) + s // 2)
            deal(s, i, (1 - side) * half + turned)
            return carry

        lax.fori_loop(0, half, step, 0)

    def deal_near(i, theirs):
        first = half if not theirs else groups if i == 0 else 0

        def step(s, carry):
            deal(first + s, i, side * half + lax.rem(g + s + 1, half), theirs)
            return carry

        lax.fori_loop(0, half - 1, step, 0)
        deal(first + half - 1, i, g, theirs, True)

    def halo(src, buf, i, to):
        return pltpu.make_async_remote_copy(
            src_ref=src,
            dst_ref=buf.at[pl.ds(0, REACH)],
            send_sem=halo_send.at[i],
            recv_sem=halo_recv.at[i],
            device_id=(to, p),
            device_id_type=MESH,
        )

    following = jnp.minimum(g + 1, groups - 1)
    preceding = jnp.maximum(g - 1, 0)
    gives_halo = (g != 1) & (g != half - 1) & (g < groups - 1)
    bufs = (kbuf, vbuf)
    halos = [halo(buf.at[pl.ds(rows, REACH)], buf, i, following) for i, buf in enumerate(bufs)]
    passed_relay = [halo(relay_ref.at[i], buf, 2 + i, preceding) for i, buf in enumerate(bufs)]
    passed_raw = [
        halo(buf.at[pl.ds(2 * rows, REACH)], buf, 2 + i, preceding)
        for i, buf in enumerate(bufs)
    ]
    gets_passed = (g == 2) | (g == half)
    gives_values = gives_halo & (g != half + 1)
    passes_across = g == half
    gets_across = g == half + 2
    to_across = pltpu.make_async_remote_copy(
        src_ref=vbuf.at[pl.ds(rows, REACH)],
        dst_ref=relay_ref.at[1],
        send_sem=relay_send.at[1],
        recv_sem=relay_recv.at[1],
        device_id=(preceding, p),
        device_id_type=MESH,
    )
    passed_across = halo(relay_ref.at[1], vbuf, 4, jnp.minimum(g + 2, groups - 1))

    @pl.when(gives_halo)
    def _():
        halos[0].start()

    @pl.when(gives_values)
    def _():
        halos[1].start()

    @pl.when(passes_raw)
    def _():
        to_across.start()

    late_far = g == 1
    soon_far = outer & jnp.logical_not(late_far)

    deal_near(1, False)

    @pl.when(soon_far)
    def _():
        deal_far(1)

    deal_near(0, False)

    @pl.when(soon_far)
    def _():
        deal_far(0)

    @pl.when(inner & jnp.logical_not(gives_raw))
    def _():
        raw_v_high.wait_send()
        raw_v_low.wait_send()

    @pl.when(inner & jnp.logical_not(gives_raw))
    def _():
        deal_far(0)

    @pl.when(g == 0)
    def _():
        kbuf[:REACH, :] = jnp.zeros((REACH, width), jnp.bfloat16)
        vbuf[:REACH, :] = jnp.zeros((REACH, width), jnp.bfloat16)

    q_in.wait()

    def pass_relay():
        for copy in to_relay:
            copy.wait_recv()
        for copy in passed_relay:
            copy.start()

    def pass_across():
        to_across.wait_recv()
        passed_across.start()

    def pass_raw():
        raw_k_high.wait_recv()
        raw_v_high.wait_recv()
        for copy in passed_raw:
            copy.start()

    def deal_their_values():
        @pl.when(jnp.logical_not(passes_raw))
        def _():
            raw_v_high.wait_recv()

        raw_v_low.wait_recv()
        raw_slots.wait_recv()
        deal_near(1, True)

    def deal_their_keys():
        raw_k_low.wait_recv()
        deal_near(0, True)

    def give_turn():
        raw_v_high.wait_send()
        raw_v_low.wait_send()
        raw_k_high.wait_send()
        raw_k_low.wait_send()
        above = jnp.maximum(g - 2, 0)
        pl.semaphore_signal(turn_sem, inc=1, device_id=(above, p), device_id_type=MESH)

    def late_deal():
        pl.semaphore_wait(turn_sem, 1)
        deal_far(1)
        deal_far(0)

    errands = (
        (GIVE_AT, gives_raw, give_turn),
        (LATE_AT, late_far, late_deal),
        (PASS_AT, passes_relay, pass_relay),
        (PASS_AT, passes_raw, pass_raw),
        (PASS_AT, passes_across, pass_across),
        (THEIRS_AT, inner, deal_their_values),
        (KEYS_AT, passes_raw, deal_their_keys),
    )

    factor = HEAD_DIM**-0.5 * math.log2(math.e)
    ahead = steps - REACH // TILE

    def attend(it, carry):
        b = lax.rem(it + REACH // TILE, steps)
        start = pl.multiple_of(b * TILE, TILE)

        for turn_at, whose, action in errands:
            if turn_at < steps:
                pl.when((it == turn_at) & whose)(action)

        @pl.when((it == ahead) & (g > 0) & jnp.logical_not(gets_passed))
        def _():
            halos[0].wait_recv()

        @pl.when((it == ahead) & (g > 0) & jnp.logical_not(gets_passed | gets_across))
        def _():
            halos[1].wait_recv()

        @pl.when((it == ahead) & gets_across)
        def _():
            passed_across.wait_recv()

        @pl.when((it == ahead) & gets_passed)
        def _():
            for copy in passed_raw:
                copy.wait_recv()

        mask = allowed(b)
        cosine = cos_ref[pl.ds(start, TILE), :]
        sine = sin_ref[pl.ds(start, TILE), :]
        for h in range(key_heads):
            cols = slice(h * HEAD_DIM, (h + 1) * HEAD_DIM)
            keys = kbuf[pl.ds(start, window), cols]
            vals = vbuf[pl.ds(start, window), cols]
            for part in range(0, rep, 4):
                lanes = [
                    slice((h * rep + r) * HEAD_DIM, (h * rep + r + 1) * HEAD_DIM)
                    for r in range(part, part + 4)
                ]
                q = jnp.concatenate(
                    [
                        turn(qbuf[pl.ds(start, TILE), lane].astype(jnp.float32), cosine, sine)
                        for lane in lanes
                    ],
                    0,
                )
                scores = lax.dot_general(
                    q, keys, (((1,), (1,)), ((), ())), preferred_element_type=jnp.float32
                )
                scores = scores.reshape(4, TILE, window)
                scores = jnp.where(mask[None], scores * factor, -1e30)
                expo = jnp.exp2(scores - jnp.max(scores, -1, keepdims=True))
                total = jnp.sum(expo, -1, keepdims=True)
                mixed = jnp.dot(
                    expo.reshape(4 * TILE, window).astype(jnp.bfloat16),
                    vals,
                    preferred_element_type=jnp.float32,
                ).reshape(4, TILE, HEAD_DIM)
                mixed = (mixed / total).astype(jnp.bfloat16)
                for r, lane in enumerate(lanes):
                    obuf[pl.ds(start, TILE), lane] = mixed[r]
        return carry

    lax.fori_loop(0, steps, attend, 0)
    out = pltpu.make_async_copy(obuf, attn_hbm, out_sem)
    out.start()

    for turn_at, whose, action in errands:
        if turn_at >= steps:
            pl.when(whose)(action)

    @pl.when(inner)
    def _():
        raw_slots.wait_send()

    @pl.when(gives_halo)
    def _():
        halos[0].wait_send()

    @pl.when(gives_values)
    def _():
        halos[1].wait_send()

    @pl.when(passes_across)
    def _():
        passed_across.wait_send()

    @pl.when(relays)
    def _():
        for copy in to_relay:
            copy.wait_send()

    @pl.when(passes_relay)
    def _():
        for copy in passed_relay:
            copy.wait_send()

    @pl.when(passes_raw)
    def _():
        to_across.wait_send()
        for copy in passed_raw:
            copy.wait_send()

    blocks = groups * tps
    for i, (_, send, cache) in enumerate(lanes_of):

        def wait_sent(count):
            sent = send.at[pl.ds(0, count)]
            pltpu.make_async_copy(sent, sent, send_sem.at[i]).wait()

        if i == 0:
            few = half * tps - 1
            pl.when(gives_raw)(functools.partial(wait_sent, few))
            pl.when(passes_raw)(functools.partial(wait_sent, blocks + few - 1))
            plain = jnp.logical_not(gives_raw | passes_raw)
            pl.when(plain)(functools.partial(wait_sent, blocks - 1))
        else:
            pl.when(outer)(functools.partial(wait_sent, blocks - 1))
            pl.when(inner)(functools.partial(wait_sent, blocks - 2))
        pltpu.make_async_copy(cache, cache, recv_sem.at[i]).wait()
    out.wait()


def hand_over(*arrays):
    count, pieces = len(arrays), 4

    def copy_kernel(*refs):
        sem = refs[-1]
        copies = []
        for i in range(count):
            piece = arrays[i].shape[0] // pieces
            for j in range(pieces):
                part = pl.ds(j * piece, piece)
                copies.append(
                    pltpu.make_async_copy(
                        refs[i].at[part], refs[count + i].at[part], sem.at[i, j]
                    )
                )
        for copy in copies:
            copy.start()
        for copy in copies:
            copy.wait()

    anywhere = pl.BlockSpec(memory_space=pl.ANY)
    return pl.pallas_call(
        copy_kernel,
        out_shape=tuple(jax.ShapeDtypeStruct(a.shape, a.dtype) for a in arrays),
        in_specs=[anywhere] * count,
        out_specs=(anywhere,) * count,
        scratch_shapes=[pltpu.SemaphoreType.DMA((count, pieces))],
        compiler_params=pltpu.CompilerParams(vmem_limit_bytes=16 * 2**20),
    )(*arrays)


def shards(queries, keys, values, segment_ids, cache_owner):
    rows, width = keys.shape
    groups = lax.axis_size("grp")
    tps = lax.axis_size("tp")
    cap = max(1, rows // (2 * groups))
    if cap % 16 or rows % TILE or rows < 2 * REACH or groups != 8:
        return plain_shards(queries, keys, values, segment_ids, cache_owner)
    anywhere = pl.BlockSpec(memory_space=pl.ANY)
    hbm = pl.BlockSpec(memory_space=pltpu.HBM)
    bf16 = jnp.bfloat16
    table = jnp.asarray(rope_table())
    cache = jax.ShapeDtypeStruct((groups * cap, tps * width), bf16)
    landed = pl.pallas_call(
        functools.partial(kernel, groups, tps, cap),
        out_shape=(jax.ShapeDtypeStruct(queries.shape, bf16), cache, cache),
        in_specs=[hbm] * 6,
        out_specs=(anywhere, anywhere, anywhere),
        scratch_shapes=[
            pltpu.VMEM(queries.shape, bf16),
            pltpu.VMEM((rows, width), bf16),
            pltpu.VMEM((REACH + 2 * rows, width), bf16),
            pltpu.VMEM((REACH + 2 * rows, width), bf16),
            pltpu.VMEM((groups * tps + groups // 2 * tps, cap, width), bf16),
            pltpu.VMEM((groups * tps, cap, width), bf16),
            pltpu.VMEM(queries.shape, bf16),
            pltpu.VMEM((rows, HEAD_DIM), jnp.float32),
            pltpu.VMEM((rows, HEAD_DIM), jnp.float32),
            pltpu.VMEM((1, REACH + rows), jnp.float32),
            pltpu.VMEM((rows, TILE), jnp.float32),
            pltpu.VMEM((2, 1, rows), jnp.int32),
            pltpu.VMEM(table.shape, bf16),
            pltpu.VMEM((1, segment_ids.shape[0]), jnp.int32),
            pltpu.VMEM((1, rows), jnp.int32),
            pltpu.SemaphoreType.DMA((6,)),
            pltpu.SemaphoreType.DMA,
            pltpu.SemaphoreType.DMA((2,)),
            pltpu.SemaphoreType.DMA((2,)),
            pltpu.SemaphoreType.DMA((5,)),
            pltpu.SemaphoreType.DMA((5,)),
            pltpu.SemaphoreType.DMA((5,)),
            pltpu.SemaphoreType.DMA((5,)),
            pltpu.VMEM((2, REACH, width), bf16),
            pltpu.SemaphoreType.DMA((2,)),
            pltpu.SemaphoreType.DMA((2,)),
            pltpu.SemaphoreType.REGULAR,
            pltpu.SemaphoreType.REGULAR,
        ],
        compiler_params=pltpu.CompilerParams(
            collective_id=0, has_side_effects=True, vmem_limit_bytes=40 * 2**20
        ),
    )(
        *(
            pltpu.with_memory_space_constraint(operand, pltpu.HBM)
            for operand in (
                queries,
                keys,
                values,
                table,
                segment_ids.reshape(1, -1),
                cache_owner.reshape(1, -1),
            )
        )
    )
    return hand_over(*landed)


def solution(mesh):
    in_specs = (P("grp", "tp"), P("grp", "tp"), P("grp", "tp"), P(), P("grp", None))
    out_specs = (P("grp", "tp"), P(("grp", "tp"), None), P(("grp", "tp"), None))
    return jax.shard_map(shards, mesh=mesh, in_specs=in_specs, out_specs=out_specs, check_vma=False)
```

```python
import functools
import math

import jax
import jax.numpy as jnp
import ml_dtypes
import numpy as np
from jax import lax
from jax.experimental import pallas as pl
from jax.experimental.pallas import tpu as pltpu
from jax.sharding import PartitionSpec as P

HEAD_DIM = 128
REACH = 256
TILE = 128
MESH = pl.DeviceIdType.MESH
PASS_AT = 0
LATE_AT = 2
GIVE_AT = 2
THEIRS_AT = 2
KEYS_AT = 4


rope_base = 10000.0


def shifted(block, axis, distance):
    devices = range(lax.axis_size(axis))
    route = [(i - distance, i) for i in devices if i - distance in devices]
    return lax.ppermute(block, axis, route)


def earlier_alike(labels):
    alike = labels[:, None] == labels[None, :]
    order = jnp.arange(labels.shape[0], dtype=jnp.int32)
    return jnp.sum((alike & (order[None, :] < order[:, None])).astype(jnp.int32), 1)


def rotate(tensor, places):
    half_dim = tensor.shape[-1] // 2
    inverse = jnp.exp(
        jnp.arange(half_dim, dtype=jnp.float32) * (-2.0 * math.log(rope_base) / tensor.shape[-1])
    )
    angles = places.astype(jnp.float32)[:, None] * inverse[None, :]
    cosine = jnp.cos(angles)[:, None, :]
    sine_part = jnp.sin(angles)[:, None, :]
    first_half = tensor[..., :half_dim].astype(jnp.float32)
    second_half = tensor[..., half_dim:].astype(jnp.float32)
    joined = jnp.concatenate(
        [
            first_half * cosine - second_half * sine_part,
            second_half * cosine + first_half * sine_part,
        ],
        -1,
    )
    return joined.astype(jnp.bfloat16)


def plain_shards(queries, keys, values, segment_ids, cache_owner):
    block_rows = queries.shape[0]
    key_width = keys.shape[1]
    query_heads = queries.shape[1] // HEAD_DIM
    key_heads = key_width // HEAD_DIM
    group_size = query_heads // key_heads
    scale = HEAD_DIM ** (-0.5)
    groups = lax.axis_size("grp")
    tp_count = lax.axis_size("tp")
    group_index = lax.axis_index("grp")
    quarter_cap = max(1, block_rows // (2 * groups))
    own_labels = lax.dynamic_slice_in_dim(segment_ids, group_index * block_rows, block_rows, 0)
    prior_labels = lax.dynamic_slice_in_dim(
        segment_ids, jnp.maximum(group_index - 1, 0) * block_rows, block_rows, 0
    )
    has_prior = group_index > 0
    carried = jnp.where(has_prior, jnp.sum((prior_labels == own_labels[0]).astype(jnp.int32)), 0)
    places = earlier_alike(own_labels) + jnp.where(own_labels == own_labels[0], carried, 0)
    q_rot = rotate(queries.reshape(block_rows, query_heads, HEAD_DIM), places)
    k_rot = rotate(keys.reshape(block_rows, key_heads, HEAD_DIM), places).reshape(
        block_rows, key_width
    )
    prior_keys, prior_values = shifted((k_rot, values), "grp", 1)
    row_index = jnp.arange(block_rows, dtype=jnp.int32)[:, None]
    column_index = jnp.arange(block_rows, dtype=jnp.int32)[None, :]
    local_mask = (own_labels[:, None] == own_labels[None, :]) & (column_index <= row_index)
    prior_mask = (own_labels[:, None] == prior_labels[None, :]) & has_prior

    def head_major(rows_flat):
        return rows_flat.reshape(-1, key_heads, HEAD_DIM).transpose(1, 0, 2)

    local_key_stack = head_major(k_rot)
    local_value_stack = head_major(values)
    prior_key_stack = head_major(prior_keys)
    prior_value_stack = head_major(prior_values)
    joint_mask = jnp.concatenate([prior_mask, local_mask], 1)
    joint_key_stack = jnp.concatenate([prior_key_stack, local_key_stack], 1)
    joint_value_stack = jnp.concatenate([prior_value_stack, local_value_stack], 1)
    query_stack = q_rot.transpose(1, 0, 2)
    head_source = jnp.arange(query_heads, dtype=jnp.int32) // group_size

    def attend(pieces):
        query_rows, source_head = pieces
        key_rows = lax.dynamic_index_in_dim(joint_key_stack, source_head, 0, keepdims=False)
        value_rows = lax.dynamic_index_in_dim(joint_value_stack, source_head, 0, keepdims=False)
        scores = (
            jnp.einsum("td,ud->tu", query_rows, key_rows, preferred_element_type=jnp.float32)
            * scale
        )
        masked = jnp.where(joint_mask, scores, -1e30)
        row_max = jnp.max(masked, -1, keepdims=True)
        expo_terms = jnp.where(joint_mask, jnp.exp(masked - row_max), 0.0)
        weights = (expo_terms / jnp.sum(expo_terms, -1, keepdims=True)).astype(jnp.bfloat16)
        mixed = jnp.dot(weights, value_rows, preferred_element_type=jnp.float32)
        return mixed.astype(jnp.bfloat16)

    head_outputs = lax.map(attend, (query_stack, head_source))
    attention = head_outputs.transpose(1, 0, 2).reshape(block_rows, query_heads * HEAD_DIM)
    owners = cache_owner[:, 0]
    ranks = earlier_alike(owners)
    send_slot = owners * (tp_count * quarter_cap) + ranks
    buffer_rows = groups * tp_count * quarter_cap
    send_keys = jnp.zeros((buffer_rows, key_width), jnp.bfloat16).at[send_slot].set(k_rot)
    send_values = jnp.zeros((buffer_rows, key_width), jnp.bfloat16).at[send_slot].set(values)
    send_keys = send_keys.reshape(groups, tp_count, quarter_cap, key_width)
    send_values = send_values.reshape(groups, tp_count, quarter_cap, key_width)
    middle_keys, middle_values = (
        lax.all_to_all(send_keys, "tp", split_axis=1, concat_axis=3, tiled=True),
        lax.all_to_all(send_values, "tp", split_axis=1, concat_axis=3, tiled=True),
    )
    got_keys, got_values = (
        lax.all_to_all(middle_keys, "grp", split_axis=0, concat_axis=0, tiled=True),
        lax.all_to_all(middle_values, "grp", split_axis=0, concat_axis=0, tiled=True),
    )
    key_cache = got_keys.reshape(groups * quarter_cap, tp_count * key_width)
    value_cache = got_values.reshape(groups * quarter_cap, tp_count * key_width)
    return (attention, key_cache, value_cache)


def rope_table():
    half_dim = HEAD_DIM // 2
    inverse = np.exp(
        np.arange(half_dim, dtype=np.float32) * np.float32(-2.0 * math.log(rope_base) / HEAD_DIM)
    ).astype(np.float32)
    angles = (np.arange(REACH, dtype=np.float32)[:, None] * inverse[None, :]).astype(np.float32)
    cosine = np.cos(angles.astype(np.float64))
    sine = np.sin(angles.astype(np.float64))
    rest = np.concatenate([cosine, cosine, -sine, sine], 1)
    parts = []
    for _ in range(3):
        part = rest.astype(np.float32).astype(ml_dtypes.bfloat16)
        parts.append(part)
        rest = rest - part.astype(np.float64)
    return np.concatenate(parts, 1)


def kernel(
    groups,
    tps,
    cap,
    q_hbm,
    k_hbm,
    v_hbm,
    table_hbm,
    labels_hbm,
    owner_hbm,
    attn_hbm,
    kc_hbm,
    vc_hbm,
    qbuf,
    kraw,
    kbuf,
    vbuf,
    ksend,
    vsend,
    obuf,
    cos_ref,
    sin_ref,
    lab_row,
    lab_col,
    slot_ref,
    table_ref,
    labels_ref,
    owner_ref,
    in_sem,
    out_sem,
    send_sem,
    recv_sem,
    halo_send,
    halo_recv,
    raw_send,
    raw_recv,
    relay_ref,
    relay_send,
    relay_recv,
    ready_sem,
    turn_sem,
):
    rows, width = kraw.shape
    key_heads = width // HEAD_DIM
    q_heads = qbuf.shape[1] // HEAD_DIM
    rep = q_heads // key_heads
    steps = rows // TILE
    window = REACH + TILE
    half = groups // 2
    g = lax.axis_index("grp")
    p = lax.axis_index("tp")
    side = g // half
    y = lax.rem(g, 2)
    first_layer = g < 2
    last_layer = g >= groups - 2
    outer = first_layer | last_layer
    inner = jnp.logical_not(outer)
    partner = jnp.where(side == 0, jnp.minimum(g + 2, groups - 1), jnp.maximum(g - 2, 0))
    own_start = REACH
    partner_start = REACH + rows

    barrier = pltpu.get_barrier_semaphore()

    @pl.when(inner)
    def _():
        pl.semaphore_signal(barrier, inc=1, device_id=(partner, p), device_id_type=MESH)

    @pl.when(inner & (side == 0))
    def _():
        above = jnp.maximum(g - 2, 0)
        pl.semaphore_signal(barrier, inc=1, device_id=(above, p), device_id_type=MESH)

    arrivals = [
        pltpu.make_async_copy(src, dst, in_sem.at[i])
        for i, (src, dst) in enumerate(
            (
                (owner_hbm, owner_ref),
                (labels_hbm, labels_ref),
                (k_hbm, kraw),
                (table_hbm, table_ref),
                (v_hbm, vbuf.at[pl.ds(own_start, rows)]),
                (q_hbm, qbuf),
            )
        )
    ]
    for arrival in arrivals:
        arrival.start()
    owner_in, labels_in, k_in, table_in, v_in, q_in = arrivals

    def greet(i, carry):
        there = groups - 2 + i // tps
        seat = lax.rem(i, tps)

        @pl.when((there != g) | (seat != p))
        def _():
            pl.semaphore_signal(
                barrier, inc=1, device_id=(there, seat), device_id_type=MESH
            )

        return carry

    lax.fori_loop(0, 2 * tps, greet, 0)

    def raw(i, src, dst):
        return pltpu.make_async_remote_copy(
            src_ref=src,
            dst_ref=dst,
            send_sem=raw_send.at[i],
            recv_sem=raw_recv.at[i],
            device_id=(partner, p),
            device_id_type=MESH,
        )

    low, high = rows - REACH, REACH
    raw_v_high = raw(
        0, v_hbm.at[pl.ds(low, high)], vbuf.at[pl.ds(partner_start + low, high)]
    )
    raw_v_low = raw(1, v_hbm.at[pl.ds(0, low)], vbuf.at[pl.ds(partner_start, low)])
    raw_slots = raw(2, slot_ref.at[0], slot_ref.at[1])
    raw_k_high = raw(
        3, kbuf.at[pl.ds(own_start + low, high)], kbuf.at[pl.ds(partner_start + low, high)]
    )
    cut = low - 32
    raw_k_low = raw(4, kbuf.at[pl.ds(own_start, cut)], kbuf.at[pl.ds(partner_start, cut)])
    raw_k_last = raw(
        5,
        kbuf.at[pl.ds(own_start + cut, low - cut)],
        kbuf.at[pl.ds(partner_start + cut, low - cut)],
    )
    gives_raw = g == half - 1
    passes_raw = g == half + 1

    relays = g == 1
    passes_relay = g == half - 1
    to_relay = [
        pltpu.make_async_remote_copy(
            src_ref=src,
            dst_ref=relay_ref.at[i],
            send_sem=relay_send.at[i],
            recv_sem=relay_recv.at[i],
            device_id=(jnp.minimum(g + 2, groups - 1), p),
            device_id_type=MESH,
        )
        for i, src in enumerate((kbuf.at[pl.ds(rows, REACH)], v_hbm.at[pl.ds(low, high)]))
    ]

    @pl.when(jnp.logical_not(last_layer))
    def _():
        pl.semaphore_wait(barrier, 1)

    @pl.when(inner)
    def _():
        raw_v_high.start()

    @pl.when(relays)
    def _():
        to_relay[1].start()

    @pl.when(last_layer)
    def _():
        pl.semaphore_wait(barrier, groups * tps - 1)
        for layer in range(1, groups // 2):
            below = jnp.maximum(g - 2 * layer, 0)
            pl.semaphore_signal(ready_sem, inc=1, device_id=(below, p), device_id_type=MESH)

    owner_in.wait()
    owners = owner_ref[...]
    owner_pad = -(-groups // 16) * 16
    one_hot = (lax.broadcasted_iota(jnp.int32, (owner_pad, rows), 0) == owners).astype(jnp.float32)
    earlier = (
        lax.broadcasted_iota(jnp.int32, (rows, rows), 0)
        < lax.broadcasted_iota(jnp.int32, (rows, rows), 1)
    ).astype(jnp.float32)
    counts = jnp.dot(
        one_hot.astype(jnp.bfloat16),
        earlier.astype(jnp.bfloat16),
        preferred_element_type=jnp.float32,
    )
    ranks = jnp.sum(counts * one_hot, 0, keepdims=True)
    slot_ref[0] = owners * (tps * cap) + ranks.astype(jnp.int32)

    @pl.when(inner)
    def _():
        raw_slots.start()

    def allowed(b):
        start = pl.multiple_of(b * TILE, TILE)
        line = lab_row[:, pl.ds(start, window)]
        col = lab_col[pl.ds(start, TILE), :]
        col = jnp.concatenate([col] * (window // TILE), 1)
        causal = (
            lax.broadcasted_iota(jnp.int32, (TILE, window), 1)
            <= lax.broadcasted_iota(jnp.int32, (TILE, window), 0) + REACH
        )
        return (col == line) & causal

    def turn(x, cosine, sine):
        return (x * cosine + pltpu.roll(x, HEAD_DIM // 2, 1) * sine).astype(jnp.bfloat16)

    labels_in.wait()
    k_in.wait()
    table_in.wait()
    before = pl.multiple_of(jnp.maximum(g * rows - REACH, 0), 128)
    prior = labels_ref[:, pl.ds(before, REACH)].astype(jnp.float32)
    own = labels_ref[:, pl.ds(pl.multiple_of(g * rows, 128), rows)].astype(jnp.float32)
    lab_row[:, :REACH] = jnp.where(jnp.full(prior.shape, g) > 0, prior, -1.0)
    lab_row[:, REACH:] = own
    for b in range(steps):
        line = own[:, b * TILE : (b + 1) * TILE]
        lab_col[pl.ds(b * TILE, TILE), :] = jnp.transpose(jnp.broadcast_to(line, (TILE, TILE)))

    def rotate_keys(b, carry):
        start = pl.multiple_of(b * TILE, TILE)
        place = jnp.sum(allowed(b).astype(jnp.float32), 1, keepdims=True) - 1.0
        pick = lax.broadcasted_iota(jnp.int32, (TILE, REACH), 1) == place.astype(jnp.int32)
        pick = pick.astype(jnp.float32).astype(jnp.bfloat16)
        found = jnp.dot(pick, table_ref[...], preferred_element_type=jnp.float32)
        wide = 2 * HEAD_DIM
        found = found[:, :wide] + found[:, wide : 2 * wide] + found[:, 2 * wide :]
        cosine, sine = found[:, :HEAD_DIM], found[:, HEAD_DIM:]
        cos_ref[pl.ds(start, TILE), :] = cosine
        sin_ref[pl.ds(start, TILE), :] = sine
        for h in range(key_heads):
            cols = slice(h * HEAD_DIM, (h + 1) * HEAD_DIM)
            x = kraw[pl.ds(start, TILE), cols].astype(jnp.float32)
            kbuf[pl.ds(pl.multiple_of(own_start + start, TILE), TILE), cols] = turn(x, cosine, sine)
        return carry

    lax.fori_loop(0, steps, rotate_keys, 0)

    @pl.when(gives_raw)
    def _():
        raw_k_high.start()

    @pl.when(inner)
    def _():
        raw_v_low.start()

    @pl.when(gives_raw)
    def _():
        raw_k_low.start()
        raw_k_last.start()

    @pl.when(relays)
    def _():
        to_relay[0].start()

    v_in.wait()

    @pl.when(jnp.logical_not(last_layer))
    def _():
        pl.semaphore_wait(ready_sem, 1)

    lanes_of = ((kbuf, ksend, kc_hbm), (vbuf, vsend, vc_hbm))
    land_cols = pl.ds(pl.multiple_of(p * width, width), width)

    def deal(unit, i, owner, theirs=False, mine=False):
        buf, send, cache = lanes_of[i]
        source = partner if theirs else g
        first = partner_start if theirs else own_start
        land = cache.at[pl.ds(pl.multiple_of(source * cap, cap), cap), land_cols]
        slots = lax.broadcasted_iota(jnp.int32, (tps * cap, rows), 0) + owner * (tps * cap)
        pick = (slots == slot_ref[int(theirs)]).astype(jnp.float32).astype(jnp.bfloat16)
        got = jnp.dot(pick, buf[pl.ds(first, rows), :], preferred_element_type=jnp.float32)
        send[pl.ds(unit * tps, tps)] = got.astype(jnp.bfloat16).reshape(tps, cap, width)
        for j in range(int(mine), tps):
            quarter = lax.rem(p + j, tps) if mine else j
            pltpu.make_async_remote_copy(
                src_ref=send.at[unit * tps + quarter],
                dst_ref=land,
                send_sem=send_sem.at[i],
                recv_sem=recv_sem.at[i],
                device_id=(owner, quarter),
                device_id_type=MESH,
            ).start()
        if mine:
            pltpu.make_async_copy(send.at[unit * tps + p], land, recv_sem.at[i]).start()

    def deal_far(i):
        def step(s, carry):
            turned = jnp.where(side == 0, 2 - 2 * lax.rem(s, 2) + s // 2, s)
            deal(s, i, (1 - side) * half + turned)
            return carry

        lax.fori_loop(0, half, step, 0)

    def deal_near(i, theirs):
        first = half if not theirs else groups if i == 0 else 0

        def step(s, carry):
            deal(first + s, i, side * half + lax.rem(g + s + 1, half), theirs)
            return carry

        lax.fori_loop(0, half - 1, step, 0)
        deal(first + half - 1, i, g, theirs, True)

    def halo(src, buf, i, to):
        return pltpu.make_async_remote_copy(
            src_ref=src,
            dst_ref=buf.at[pl.ds(0, REACH)],
            send_sem=halo_send.at[i],
            recv_sem=halo_recv.at[i],
            device_id=(to, p),
            device_id_type=MESH,
        )

    following = jnp.minimum(g + 1, groups - 1)
    preceding = jnp.maximum(g - 1, 0)
    gives_halo = (g != 1) & (g != half - 1) & (g < groups - 1)
    bufs = (kbuf, vbuf)
    halos = [halo(buf.at[pl.ds(rows, REACH)], buf, i, following) for i, buf in enumerate(bufs)]
    passed_relay = [halo(relay_ref.at[i], buf, 2 + i, preceding) for i, buf in enumerate(bufs)]
    passed_raw = [
        halo(buf.at[pl.ds(2 * rows, REACH)], buf, 2 + i, preceding)
        for i, buf in enumerate(bufs)
    ]
    gets_passed = (g == 2) | (g == half)
    gives_values = gives_halo & (g != half + 1)
    passes_across = g == half
    gets_across = g == half + 2
    to_across = pltpu.make_async_remote_copy(
        src_ref=vbuf.at[pl.ds(rows, REACH)],
        dst_ref=relay_ref.at[1],
        send_sem=relay_send.at[1],
        recv_sem=relay_recv.at[1],
        device_id=(preceding, p),
        device_id_type=MESH,
    )
    passed_across = halo(relay_ref.at[1], vbuf, 4, jnp.minimum(g + 2, groups - 1))

    @pl.when(gives_halo)
    def _():
        halos[0].start()

    @pl.when(gives_values)
    def _():
        halos[1].start()

    @pl.when(passes_raw)
    def _():
        to_across.start()

    late_far = g == 1
    soon_far = outer & jnp.logical_not(late_far)

    deal_near(1, False)

    @pl.when(soon_far)
    def _():
        deal_far(1)

    deal_near(0, False)

    @pl.when(soon_far)
    def _():
        deal_far(0)

    @pl.when(inner & jnp.logical_not(gives_raw))
    def _():
        raw_v_high.wait_send()
        raw_v_low.wait_send()

    @pl.when(inner & jnp.logical_not(gives_raw))
    def _():
        deal_far(0)

    @pl.when(g == 0)
    def _():
        kbuf[:REACH, :] = jnp.zeros((REACH, width), jnp.bfloat16)
        vbuf[:REACH, :] = jnp.zeros((REACH, width), jnp.bfloat16)

    q_in.wait()

    def pass_relay():
        for copy in to_relay:
            copy.wait_recv()
        for copy in passed_relay:
            copy.start()

    def pass_across():
        to_across.wait_recv()
        passed_across.start()

    def pass_raw():
        raw_k_high.wait_recv()
        raw_v_high.wait_recv()
        for copy in passed_raw:
            copy.start()

    def deal_their_values():
        @pl.when(jnp.logical_not(passes_raw))
        def _():
            raw_v_high.wait_recv()

        raw_v_low.wait_recv()
        raw_slots.wait_recv()
        deal_near(1, True)

    def deal_their_keys():
        raw_k_low.wait_recv()
        raw_k_last.wait_recv()
        deal_near(0, True)

    def give_turn():
        raw_v_high.wait_send()
        raw_v_low.wait_send()
        raw_k_high.wait_send()
        raw_k_low.wait_send()
        above = jnp.maximum(g - 2, 0)
        pl.semaphore_signal(turn_sem, inc=1, device_id=(above, p), device_id_type=MESH)

    def late_deal():
        pl.semaphore_wait(turn_sem, 1)
        deal_far(1)
        deal_far(0)

    errands = (
        (GIVE_AT, gives_raw, give_turn),
        (LATE_AT, late_far, late_deal),
        (PASS_AT, passes_relay, pass_relay),
        (PASS_AT, passes_raw, pass_raw),
        (PASS_AT, passes_across, pass_across),
        (THEIRS_AT, inner, deal_their_values),
        (KEYS_AT, passes_raw, deal_their_keys),
    )

    factor = HEAD_DIM**-0.5 * math.log2(math.e)
    ahead = steps - REACH // TILE

    def attend(it, carry):
        b = lax.rem(it + REACH // TILE, steps)
        start = pl.multiple_of(b * TILE, TILE)

        for turn_at, whose, action in errands:
            if turn_at < steps:
                pl.when((it == turn_at) & whose)(action)

        @pl.when((it == ahead) & (g > 0) & jnp.logical_not(gets_passed))
        def _():
            halos[0].wait_recv()

        @pl.when((it == ahead) & (g > 0) & jnp.logical_not(gets_passed | gets_across))
        def _():
            halos[1].wait_recv()

        @pl.when((it == ahead) & gets_across)
        def _():
            passed_across.wait_recv()

        @pl.when((it == ahead) & gets_passed)
        def _():
            for copy in passed_raw:
                copy.wait_recv()

        mask = allowed(b)
        cosine = cos_ref[pl.ds(start, TILE), :]
        sine = sin_ref[pl.ds(start, TILE), :]
        for h in range(key_heads):
            cols = slice(h * HEAD_DIM, (h + 1) * HEAD_DIM)
            keys = kbuf[pl.ds(start, window), cols]
            vals = vbuf[pl.ds(start, window), cols]
            for part in range(0, rep, 4):
                lanes = [
                    slice((h * rep + r) * HEAD_DIM, (h * rep + r + 1) * HEAD_DIM)
                    for r in range(part, part + 4)
                ]
                q = jnp.concatenate(
                    [
                        turn(qbuf[pl.ds(start, TILE), lane].astype(jnp.float32), cosine, sine)
                        for lane in lanes
                    ],
                    0,
                )
                scores = lax.dot_general(
                    q, keys, (((1,), (1,)), ((), ())), preferred_element_type=jnp.float32
                )
                scores = scores.reshape(4, TILE, window)
                scores = jnp.where(mask[None], scores * factor, -1e30)
                expo = jnp.exp2(scores - jnp.max(scores, -1, keepdims=True))
                total = jnp.sum(expo, -1, keepdims=True)
                mixed = jnp.dot(
                    expo.reshape(4 * TILE, window).astype(jnp.bfloat16),
                    vals,
                    preferred_element_type=jnp.float32,
                ).reshape(4, TILE, HEAD_DIM)
                mixed = (mixed / total).astype(jnp.bfloat16)
                for r, lane in enumerate(lanes):
                    obuf[pl.ds(start, TILE), lane] = mixed[r]
        return carry

    lax.fori_loop(0, steps, attend, 0)
    out = pltpu.make_async_copy(obuf, attn_hbm, out_sem)
    out.start()

    for turn_at, whose, action in errands:
        if turn_at >= steps:
            pl.when(whose)(action)

    @pl.when(inner)
    def _():
        raw_slots.wait_send()

    @pl.when(gives_halo)
    def _():
        halos[0].wait_send()

    @pl.when(gives_values)
    def _():
        halos[1].wait_send()

    @pl.when(passes_across)
    def _():
        passed_across.wait_send()

    @pl.when(relays)
    def _():
        for copy in to_relay:
            copy.wait_send()

    @pl.when(passes_relay)
    def _():
        for copy in passed_relay:
            copy.wait_send()

    @pl.when(gives_raw)
    def _():
        raw_k_last.wait_send()

    @pl.when(passes_raw)
    def _():
        to_across.wait_send()
        for copy in passed_raw:
            copy.wait_send()

    blocks = groups * tps
    for i, (_, send, cache) in enumerate(lanes_of):

        def wait_sent(count):
            sent = send.at[pl.ds(0, count)]
            pltpu.make_async_copy(sent, sent, send_sem.at[i]).wait()

        if i == 0:
            few = half * tps - 1
            pl.when(gives_raw)(functools.partial(wait_sent, few))
            pl.when(passes_raw)(functools.partial(wait_sent, blocks + few - 1))
            plain = jnp.logical_not(gives_raw | passes_raw)
            pl.when(plain)(functools.partial(wait_sent, blocks - 1))
        else:
            pl.when(outer)(functools.partial(wait_sent, blocks - 1))
            pl.when(inner)(functools.partial(wait_sent, blocks - 2))
        pltpu.make_async_copy(cache, cache, recv_sem.at[i]).wait()
    out.wait()


def hand_over(*arrays):
    count, pieces = len(arrays), 1

    def copy_kernel(*refs):
        sem = refs[-1]
        copies = []
        for i in range(count):
            piece = arrays[i].shape[0] // pieces
            for j in range(pieces):
                part = pl.ds(j * piece, piece)
                copies.append(
                    pltpu.make_async_copy(
                        refs[i].at[part], refs[count + i].at[part], sem.at[i, j]
                    )
                )
        for copy in copies:
            copy.start()
        for copy in copies:
            copy.wait()

    anywhere = pl.BlockSpec(memory_space=pl.ANY)
    return pl.pallas_call(
        copy_kernel,
        out_shape=tuple(jax.ShapeDtypeStruct(a.shape, a.dtype) for a in arrays),
        in_specs=[anywhere] * count,
        out_specs=(anywhere,) * count,
        scratch_shapes=[pltpu.SemaphoreType.DMA((count, pieces))],
        compiler_params=pltpu.CompilerParams(vmem_limit_bytes=16 * 2**20),
    )(*arrays)


def shards(queries, keys, values, segment_ids, cache_owner):
    rows, width = keys.shape
    groups = lax.axis_size("grp")
    tps = lax.axis_size("tp")
    cap = max(1, rows // (2 * groups))
    if cap % 16 or rows % TILE or rows < 2 * REACH or groups != 8:
        return plain_shards(queries, keys, values, segment_ids, cache_owner)
    anywhere = pl.BlockSpec(memory_space=pl.ANY)
    hbm = pl.BlockSpec(memory_space=pltpu.HBM)
    bf16 = jnp.bfloat16
    table = jnp.asarray(rope_table())
    cache = jax.ShapeDtypeStruct((groups * cap, tps * width), bf16)
    landed = pl.pallas_call(
        functools.partial(kernel, groups, tps, cap),
        out_shape=(jax.ShapeDtypeStruct(queries.shape, bf16), cache, cache),
        in_specs=[hbm] * 6,
        out_specs=(anywhere, anywhere, anywhere),
        scratch_shapes=[
            pltpu.VMEM(queries.shape, bf16),
            pltpu.VMEM((rows, width), bf16),
            pltpu.VMEM((REACH + 2 * rows, width), bf16),
            pltpu.VMEM((REACH + 2 * rows, width), bf16),
            pltpu.VMEM((groups * tps + groups // 2 * tps, cap, width), bf16),
            pltpu.VMEM((groups * tps, cap, width), bf16),
            pltpu.VMEM(queries.shape, bf16),
            pltpu.VMEM((rows, HEAD_DIM), jnp.float32),
            pltpu.VMEM((rows, HEAD_DIM), jnp.float32),
            pltpu.VMEM((1, REACH + rows), jnp.float32),
            pltpu.VMEM((rows, TILE), jnp.float32),
            pltpu.VMEM((2, 1, rows), jnp.int32),
            pltpu.VMEM(table.shape, bf16),
            pltpu.VMEM((1, segment_ids.shape[0]), jnp.int32),
            pltpu.VMEM((1, rows), jnp.int32),
            pltpu.SemaphoreType.DMA((6,)),
            pltpu.SemaphoreType.DMA,
            pltpu.SemaphoreType.DMA((2,)),
            pltpu.SemaphoreType.DMA((2,)),
            pltpu.SemaphoreType.DMA((6,)),
            pltpu.SemaphoreType.DMA((6,)),
            pltpu.SemaphoreType.DMA((6,)),
            pltpu.SemaphoreType.DMA((6,)),
            pltpu.VMEM((2, REACH, width), bf16),
            pltpu.SemaphoreType.DMA((2,)),
            pltpu.SemaphoreType.DMA((2,)),
            pltpu.SemaphoreType.REGULAR,
            pltpu.SemaphoreType.REGULAR,
        ],
        compiler_params=pltpu.CompilerParams(
            collective_id=0, has_side_effects=True, vmem_limit_bytes=40 * 2**20
        ),
    )(
        *(
            pltpu.with_memory_space_constraint(operand, pltpu.HBM)
            for operand in (
                queries,
                keys,
                values,
                table,
                segment_ids.reshape(1, -1),
                cache_owner.reshape(1, -1),
            )
        )
    )
    return hand_over(*landed)


def solution(mesh):
    in_specs = (P("grp", "tp"), P("grp", "tp"), P("grp", "tp"), P(), P("grp", None))
    out_specs = (P("grp", "tp"), P(("grp", "tp"), None), P(("grp", "tp"), None))
    return jax.shard_map(shards, mesh=mesh, in_specs=in_specs, out_specs=out_specs, check_vma=False)
```

```python
import functools
import math

import jax
import jax.numpy as jnp
import ml_dtypes
import numpy as np
from jax import lax
from jax.experimental import pallas as pl
from jax.experimental.pallas import tpu as pltpu
from jax.sharding import PartitionSpec as P

HEAD_DIM = 128
REACH = 256
TILE = 128
MESH = pl.DeviceIdType.MESH
PASS_AT = 0
LATE_AT = 2
GIVE_AT = 2
THEIRS_AT = 2
KEYS_AT = 4


rope_base = 10000.0


def shifted(block, axis, distance):
    devices = range(lax.axis_size(axis))
    route = [(i - distance, i) for i in devices if i - distance in devices]
    return lax.ppermute(block, axis, route)


def earlier_alike(labels):
    alike = labels[:, None] == labels[None, :]
    order = jnp.arange(labels.shape[0], dtype=jnp.int32)
    return jnp.sum((alike & (order[None, :] < order[:, None])).astype(jnp.int32), 1)


def rotate(tensor, places):
    half_dim = tensor.shape[-1] // 2
    inverse = jnp.exp(
        jnp.arange(half_dim, dtype=jnp.float32) * (-2.0 * math.log(rope_base) / tensor.shape[-1])
    )
    angles = places.astype(jnp.float32)[:, None] * inverse[None, :]
    cosine = jnp.cos(angles)[:, None, :]
    sine_part = jnp.sin(angles)[:, None, :]
    first_half = tensor[..., :half_dim].astype(jnp.float32)
    second_half = tensor[..., half_dim:].astype(jnp.float32)
    joined = jnp.concatenate(
        [
            first_half * cosine - second_half * sine_part,
            second_half * cosine + first_half * sine_part,
        ],
        -1,
    )
    return joined.astype(jnp.bfloat16)


def plain_shards(queries, keys, values, segment_ids, cache_owner):
    block_rows = queries.shape[0]
    key_width = keys.shape[1]
    query_heads = queries.shape[1] // HEAD_DIM
    key_heads = key_width // HEAD_DIM
    group_size = query_heads // key_heads
    scale = HEAD_DIM ** (-0.5)
    groups = lax.axis_size("grp")
    tp_count = lax.axis_size("tp")
    group_index = lax.axis_index("grp")
    quarter_cap = max(1, block_rows // (2 * groups))
    own_labels = lax.dynamic_slice_in_dim(segment_ids, group_index * block_rows, block_rows, 0)
    prior_labels = lax.dynamic_slice_in_dim(
        segment_ids, jnp.maximum(group_index - 1, 0) * block_rows, block_rows, 0
    )
    has_prior = group_index > 0
    carried = jnp.where(has_prior, jnp.sum((prior_labels == own_labels[0]).astype(jnp.int32)), 0)
    places = earlier_alike(own_labels) + jnp.where(own_labels == own_labels[0], carried, 0)
    q_rot = rotate(queries.reshape(block_rows, query_heads, HEAD_DIM), places)
    k_rot = rotate(keys.reshape(block_rows, key_heads, HEAD_DIM), places).reshape(
        block_rows, key_width
    )
    prior_keys, prior_values = shifted((k_rot, values), "grp", 1)
    row_index = jnp.arange(block_rows, dtype=jnp.int32)[:, None]
    column_index = jnp.arange(block_rows, dtype=jnp.int32)[None, :]
    local_mask = (own_labels[:, None] == own_labels[None, :]) & (column_index <= row_index)
    prior_mask = (own_labels[:, None] == prior_labels[None, :]) & has_prior

    def head_major(rows_flat):
        return rows_flat.reshape(-1, key_heads, HEAD_DIM).transpose(1, 0, 2)

    local_key_stack = head_major(k_rot)
    local_value_stack = head_major(values)
    prior_key_stack = head_major(prior_keys)
    prior_value_stack = head_major(prior_values)
    joint_mask = jnp.concatenate([prior_mask, local_mask], 1)
    joint_key_stack = jnp.concatenate([prior_key_stack, local_key_stack], 1)
    joint_value_stack = jnp.concatenate([prior_value_stack, local_value_stack], 1)
    query_stack = q_rot.transpose(1, 0, 2)
    head_source = jnp.arange(query_heads, dtype=jnp.int32) // group_size

    def attend(pieces):
        query_rows, source_head = pieces
        key_rows = lax.dynamic_index_in_dim(joint_key_stack, source_head, 0, keepdims=False)
        value_rows = lax.dynamic_index_in_dim(joint_value_stack, source_head, 0, keepdims=False)
        scores = (
            jnp.einsum("td,ud->tu", query_rows, key_rows, preferred_element_type=jnp.float32)
            * scale
        )
        masked = jnp.where(joint_mask, scores, -1e30)
        row_max = jnp.max(masked, -1, keepdims=True)
        expo_terms = jnp.where(joint_mask, jnp.exp(masked - row_max), 0.0)
        weights = (expo_terms / jnp.sum(expo_terms, -1, keepdims=True)).astype(jnp.bfloat16)
        mixed = jnp.dot(weights, value_rows, preferred_element_type=jnp.float32)
        return mixed.astype(jnp.bfloat16)

    head_outputs = lax.map(attend, (query_stack, head_source))
    attention = head_outputs.transpose(1, 0, 2).reshape(block_rows, query_heads * HEAD_DIM)
    owners = cache_owner[:, 0]
    ranks = earlier_alike(owners)
    send_slot = owners * (tp_count * quarter_cap) + ranks
    buffer_rows = groups * tp_count * quarter_cap
    send_keys = jnp.zeros((buffer_rows, key_width), jnp.bfloat16).at[send_slot].set(k_rot)
    send_values = jnp.zeros((buffer_rows, key_width), jnp.bfloat16).at[send_slot].set(values)
    send_keys = send_keys.reshape(groups, tp_count, quarter_cap, key_width)
    send_values = send_values.reshape(groups, tp_count, quarter_cap, key_width)
    middle_keys, middle_values = (
        lax.all_to_all(send_keys, "tp", split_axis=1, concat_axis=3, tiled=True),
        lax.all_to_all(send_values, "tp", split_axis=1, concat_axis=3, tiled=True),
    )
    got_keys, got_values = (
        lax.all_to_all(middle_keys, "grp", split_axis=0, concat_axis=0, tiled=True),
        lax.all_to_all(middle_values, "grp", split_axis=0, concat_axis=0, tiled=True),
    )
    key_cache = got_keys.reshape(groups * quarter_cap, tp_count * key_width)
    value_cache = got_values.reshape(groups * quarter_cap, tp_count * key_width)
    return (attention, key_cache, value_cache)


def rope_table():
    half_dim = HEAD_DIM // 2
    inverse = np.exp(
        np.arange(half_dim, dtype=np.float32) * np.float32(-2.0 * math.log(rope_base) / HEAD_DIM)
    ).astype(np.float32)
    angles = (np.arange(REACH, dtype=np.float32)[:, None] * inverse[None, :]).astype(np.float32)
    cosine = np.cos(angles.astype(np.float64))
    sine = np.sin(angles.astype(np.float64))
    rest = np.concatenate([cosine, cosine, -sine, sine], 1)
    parts = []
    for _ in range(3):
        part = rest.astype(np.float32).astype(ml_dtypes.bfloat16)
        parts.append(part)
        rest = rest - part.astype(np.float64)
    return np.concatenate(parts, 1)


def kernel(
    groups,
    tps,
    cap,
    q_hbm,
    k_hbm,
    v_hbm,
    table_hbm,
    labels_hbm,
    owner_hbm,
    attn_hbm,
    kc_hbm,
    vc_hbm,
    qbuf,
    kraw,
    kbuf,
    vbuf,
    ksend,
    vsend,
    obuf,
    cos_ref,
    sin_ref,
    lab_row,
    lab_col,
    slot_ref,
    table_ref,
    labels_ref,
    owner_ref,
    in_sem,
    out_sem,
    send_sem,
    recv_sem,
    halo_send,
    halo_recv,
    raw_send,
    raw_recv,
    relay_ref,
    relay_send,
    relay_recv,
    ready_sem,
    turn_sem,
):
    rows, width = kraw.shape
    key_heads = width // HEAD_DIM
    q_heads = qbuf.shape[1] // HEAD_DIM
    rep = q_heads // key_heads
    steps = rows // TILE
    window = REACH + TILE
    half = groups // 2
    g = lax.axis_index("grp")
    p = lax.axis_index("tp")
    side = g // half
    y = lax.rem(g, 2)
    first_layer = g < 2
    last_layer = g >= groups - 2
    outer = first_layer | last_layer
    inner = jnp.logical_not(outer)
    partner = jnp.where(side == 0, jnp.minimum(g + 2, groups - 1), jnp.maximum(g - 2, 0))
    own_start = REACH
    partner_start = REACH + rows

    barrier = pltpu.get_barrier_semaphore()

    @pl.when(inner)
    def _():
        pl.semaphore_signal(barrier, inc=1, device_id=(partner, p), device_id_type=MESH)

    @pl.when(inner & (side == 0))
    def _():
        above = jnp.maximum(g - 2, 0)
        pl.semaphore_signal(barrier, inc=1, device_id=(above, p), device_id_type=MESH)

    arrivals = [
        pltpu.make_async_copy(src, dst, in_sem.at[i])
        for i, (src, dst) in enumerate(
            (
                (owner_hbm, owner_ref),
                (labels_hbm, labels_ref),
                (k_hbm, kraw),
                (table_hbm, table_ref),
                (v_hbm, vbuf.at[pl.ds(own_start, rows)]),
                (q_hbm, qbuf),
            )
        )
    ]
    for arrival in arrivals:
        arrival.start()
    owner_in, labels_in, k_in, table_in, v_in, q_in = arrivals

    def greet(i, carry):
        there = groups - 2 + i // tps
        seat = lax.rem(i, tps)

        @pl.when((there != g) | (seat != p))
        def _():
            pl.semaphore_signal(
                barrier, inc=1, device_id=(there, seat), device_id_type=MESH
            )

        return carry

    lax.fori_loop(0, 2 * tps, greet, 0)

    def raw(i, src, dst):
        return pltpu.make_async_remote_copy(
            src_ref=src,
            dst_ref=dst,
            send_sem=raw_send.at[i],
            recv_sem=raw_recv.at[i],
            device_id=(partner, p),
            device_id_type=MESH,
        )

    low, high = rows - REACH, REACH
    raw_v_high = raw(
        0, v_hbm.at[pl.ds(low, high)], vbuf.at[pl.ds(partner_start + low, high)]
    )
    raw_v_low = raw(1, v_hbm.at[pl.ds(0, low)], vbuf.at[pl.ds(partner_start, low)])
    raw_slots = raw(2, slot_ref.at[0], slot_ref.at[1])
    raw_k_high = raw(
        3, kbuf.at[pl.ds(own_start + low, high)], kbuf.at[pl.ds(partner_start + low, high)]
    )
    cut = low - 48
    raw_k_low = raw(4, kbuf.at[pl.ds(own_start, cut)], kbuf.at[pl.ds(partner_start, cut)])
    raw_k_last = raw(
        5,
        kbuf.at[pl.ds(own_start + cut, low - cut)],
        kbuf.at[pl.ds(partner_start + cut, low - cut)],
    )
    gives_raw = g == half - 1
    passes_raw = g == half + 1

    relays = g == 1
    passes_relay = g == half - 1
    to_relay = [
        pltpu.make_async_remote_copy(
            src_ref=src,
            dst_ref=relay_ref.at[i],
            send_sem=relay_send.at[i],
            recv_sem=relay_recv.at[i],
            device_id=(jnp.minimum(g + 2, groups - 1), p),
            device_id_type=MESH,
        )
        for i, src in enumerate((kbuf.at[pl.ds(rows, REACH)], v_hbm.at[pl.ds(low, high)]))
    ]

    @pl.when(jnp.logical_not(last_layer))
    def _():
        pl.semaphore_wait(barrier, 1)

    @pl.when(inner)
    def _():
        raw_v_high.start()

    @pl.when(relays)
    def _():
        to_relay[1].start()

    @pl.when(last_layer)
    def _():
        pl.semaphore_wait(barrier, groups * tps - 1)
        for layer in range(1, groups // 2):
            below = jnp.maximum(g - 2 * layer, 0)
            pl.semaphore_signal(ready_sem, inc=1, device_id=(below, p), device_id_type=MESH)

    owner_in.wait()
    owners = owner_ref[...]
    owner_pad = -(-groups // 16) * 16
    one_hot = (lax.broadcasted_iota(jnp.int32, (owner_pad, rows), 0) == owners).astype(jnp.float32)
    earlier = (
        lax.broadcasted_iota(jnp.int32, (rows, rows), 0)
        < lax.broadcasted_iota(jnp.int32, (rows, rows), 1)
    ).astype(jnp.float32)
    counts = jnp.dot(
        one_hot.astype(jnp.bfloat16),
        earlier.astype(jnp.bfloat16),
        preferred_element_type=jnp.float32,
    )
    ranks = jnp.sum(counts * one_hot, 0, keepdims=True)
    slot_ref[0] = owners * (tps * cap) + ranks.astype(jnp.int32)

    @pl.when(inner)
    def _():
        raw_slots.start()

    def allowed(b):
        start = pl.multiple_of(b * TILE, TILE)
        line = lab_row[:, pl.ds(start, window)]
        col = lab_col[pl.ds(start, TILE), :]
        col = jnp.concatenate([col] * (window // TILE), 1)
        causal = (
            lax.broadcasted_iota(jnp.int32, (TILE, window), 1)
            <= lax.broadcasted_iota(jnp.int32, (TILE, window), 0) + REACH
        )
        return (col == line) & causal

    v_in.wait()

    lanes_of = ((kbuf, ksend, kc_hbm), (vbuf, vsend, vc_hbm))
    land_cols = pl.ds(pl.multiple_of(p * width, width), width)

    def deal(unit, i, owner, theirs=False, mine=False):
        buf, send, cache = lanes_of[i]
        source = partner if theirs else g
        first = partner_start if theirs else own_start
        land = cache.at[pl.ds(pl.multiple_of(source * cap, cap), cap), land_cols]
        slots = lax.broadcasted_iota(jnp.int32, (tps * cap, rows), 0) + owner * (tps * cap)
        pick = (slots == slot_ref[int(theirs)]).astype(jnp.float32).astype(jnp.bfloat16)
        got = jnp.dot(pick, buf[pl.ds(first, rows), :], preferred_element_type=jnp.float32)
        send[pl.ds(unit * tps, tps)] = got.astype(jnp.bfloat16).reshape(tps, cap, width)
        for j in range(int(mine), tps):
            quarter = lax.rem(p + j, tps) if mine else j
            pltpu.make_async_remote_copy(
                src_ref=send.at[unit * tps + quarter],
                dst_ref=land,
                send_sem=send_sem.at[i],
                recv_sem=recv_sem.at[i],
                device_id=(owner, quarter),
                device_id_type=MESH,
            ).start()
        if mine:
            pltpu.make_async_copy(send.at[unit * tps + p], land, recv_sem.at[i]).start()

    def deal_far(i):
        def step(s, carry):
            turned = jnp.where(side == 0, 2 - 2 * lax.rem(s, 2) + s // 2, s)
            deal(s, i, (1 - side) * half + turned)
            return carry

        lax.fori_loop(0, half, step, 0)

    def deal_near(i, theirs):
        first = half if not theirs else groups if i == 0 else 0

        def step(s, carry):
            deal(first + s, i, side * half + lax.rem(g + s + 1, half), theirs)
            return carry

        lax.fori_loop(0, half - 1, step, 0)
        deal(first + half - 1, i, g, theirs, True)

    @pl.when(last_layer)
    def _():
        deal_near(1, False)
        deal_far(1)

    def turn(x, cosine, sine):
        return (x * cosine + pltpu.roll(x, HEAD_DIM // 2, 1) * sine).astype(jnp.bfloat16)

    labels_in.wait()
    k_in.wait()
    table_in.wait()
    before = pl.multiple_of(jnp.maximum(g * rows - REACH, 0), 128)
    prior = labels_ref[:, pl.ds(before, REACH)].astype(jnp.float32)
    own = labels_ref[:, pl.ds(pl.multiple_of(g * rows, 128), rows)].astype(jnp.float32)
    lab_row[:, :REACH] = jnp.where(jnp.full(prior.shape, g) > 0, prior, -1.0)
    lab_row[:, REACH:] = own
    for b in range(steps):
        line = own[:, b * TILE : (b + 1) * TILE]
        lab_col[pl.ds(b * TILE, TILE), :] = jnp.transpose(jnp.broadcast_to(line, (TILE, TILE)))

    def rotate_keys(b, carry):
        start = pl.multiple_of(b * TILE, TILE)
        place = jnp.sum(allowed(b).astype(jnp.float32), 1, keepdims=True) - 1.0
        pick = lax.broadcasted_iota(jnp.int32, (TILE, REACH), 1) == place.astype(jnp.int32)
        pick = pick.astype(jnp.float32).astype(jnp.bfloat16)
        found = jnp.dot(pick, table_ref[...], preferred_element_type=jnp.float32)
        wide = 2 * HEAD_DIM
        found = found[:, :wide] + found[:, wide : 2 * wide] + found[:, 2 * wide :]
        cosine, sine = found[:, :HEAD_DIM], found[:, HEAD_DIM:]
        cos_ref[pl.ds(start, TILE), :] = cosine
        sin_ref[pl.ds(start, TILE), :] = sine
        for h in range(key_heads):
            cols = slice(h * HEAD_DIM, (h + 1) * HEAD_DIM)
            x = kraw[pl.ds(start, TILE), cols].astype(jnp.float32)
            kbuf[pl.ds(pl.multiple_of(own_start + start, TILE), TILE), cols] = turn(x, cosine, sine)
        return carry

    lax.fori_loop(0, steps, rotate_keys, 0)

    @pl.when(gives_raw)
    def _():
        raw_k_high.start()

    @pl.when(inner)
    def _():
        raw_v_low.start()

    @pl.when(gives_raw)
    def _():
        raw_k_low.start()
        raw_k_last.start()

    @pl.when(relays)
    def _():
        to_relay[0].start()


    @pl.when(jnp.logical_not(last_layer))
    def _():
        pl.semaphore_wait(ready_sem, 1)

    def halo(src, buf, i, to):
        return pltpu.make_async_remote_copy(
            src_ref=src,
            dst_ref=buf.at[pl.ds(0, REACH)],
            send_sem=halo_send.at[i],
            recv_sem=halo_recv.at[i],
            device_id=(to, p),
            device_id_type=MESH,
        )

    following = jnp.minimum(g + 1, groups - 1)
    preceding = jnp.maximum(g - 1, 0)
    gives_halo = (g != 1) & (g != half - 1) & (g < groups - 1)
    bufs = (kbuf, vbuf)
    halos = [halo(buf.at[pl.ds(rows, REACH)], buf, i, following) for i, buf in enumerate(bufs)]
    passed_relay = [halo(relay_ref.at[i], buf, 2 + i, preceding) for i, buf in enumerate(bufs)]
    passed_raw = [
        halo(buf.at[pl.ds(2 * rows, REACH)], buf, 2 + i, preceding)
        for i, buf in enumerate(bufs)
    ]
    gets_passed = (g == 2) | (g == half)
    gives_values = gives_halo & (g != half + 1)
    passes_across = g == half
    gets_across = g == half + 2
    to_across = pltpu.make_async_remote_copy(
        src_ref=vbuf.at[pl.ds(rows, REACH)],
        dst_ref=relay_ref.at[1],
        send_sem=relay_send.at[1],
        recv_sem=relay_recv.at[1],
        device_id=(preceding, p),
        device_id_type=MESH,
    )
    passed_across = halo(relay_ref.at[1], vbuf, 4, jnp.minimum(g + 2, groups - 1))

    @pl.when(gives_halo)
    def _():
        halos[0].start()

    @pl.when(gives_values)
    def _():
        halos[1].start()

    @pl.when(passes_raw)
    def _():
        to_across.start()

    late_far = g == 1
    soon_far = outer & jnp.logical_not(late_far)

    pl.when(jnp.logical_not(last_layer))(functools.partial(deal_near, 1, False))

    @pl.when(g == 0)
    def _():
        deal_far(1)

    deal_near(0, False)

    @pl.when(soon_far)
    def _():
        deal_far(0)

    @pl.when(inner & jnp.logical_not(gives_raw))
    def _():
        raw_v_high.wait_send()
        raw_v_low.wait_send()

    @pl.when(inner & jnp.logical_not(gives_raw))
    def _():
        deal_far(0)

    @pl.when(g == 0)
    def _():
        kbuf[:REACH, :] = jnp.zeros((REACH, width), jnp.bfloat16)
        vbuf[:REACH, :] = jnp.zeros((REACH, width), jnp.bfloat16)

    q_in.wait()

    def pass_relay():
        for copy in to_relay:
            copy.wait_recv()
        for copy in passed_relay:
            copy.start()

    def pass_across():
        to_across.wait_recv()
        passed_across.start()

    def pass_raw():
        raw_k_high.wait_recv()
        raw_v_high.wait_recv()
        for copy in passed_raw:
            copy.start()

    def deal_their_values():
        @pl.when(jnp.logical_not(passes_raw))
        def _():
            raw_v_high.wait_recv()

        raw_v_low.wait_recv()
        raw_slots.wait_recv()
        deal_near(1, True)

    def deal_their_keys():
        raw_k_low.wait_recv()
        raw_k_last.wait_recv()
        deal_near(0, True)

    def give_turn():
        raw_v_high.wait_send()
        raw_v_low.wait_send()
        raw_k_high.wait_send()
        raw_k_low.wait_send()
        above = jnp.maximum(g - 2, 0)
        pl.semaphore_signal(turn_sem, inc=1, device_id=(above, p), device_id_type=MESH)

    def late_deal():
        pl.semaphore_wait(turn_sem, 1)
        deal_far(1)
        deal_far(0)

    errands = (
        (GIVE_AT, gives_raw, give_turn),
        (LATE_AT, late_far, late_deal),
        (PASS_AT, passes_relay, pass_relay),
        (PASS_AT, passes_raw, pass_raw),
        (PASS_AT, passes_across, pass_across),
        (THEIRS_AT, inner, deal_their_values),
        (KEYS_AT, passes_raw, deal_their_keys),
    )

    factor = HEAD_DIM**-0.5 * math.log2(math.e)
    ahead = steps - REACH // TILE

    def attend(it, carry):
        b = lax.rem(it + REACH // TILE, steps)
        start = pl.multiple_of(b * TILE, TILE)

        for turn_at, whose, action in errands:
            if turn_at < steps:
                pl.when((it == turn_at) & whose)(action)

        @pl.when((it == ahead) & (g > 0) & jnp.logical_not(gets_passed))
        def _():
            halos[0].wait_recv()

        @pl.when((it == ahead) & (g > 0) & jnp.logical_not(gets_passed | gets_across))
        def _():
            halos[1].wait_recv()

        @pl.when((it == ahead) & gets_across)
        def _():
            passed_across.wait_recv()

        @pl.when((it == ahead) & gets_passed)
        def _():
            for copy in passed_raw:
                copy.wait_recv()

        mask = allowed(b)
        cosine = cos_ref[pl.ds(start, TILE), :]
        sine = sin_ref[pl.ds(start, TILE), :]
        for h in range(key_heads):
            cols = slice(h * HEAD_DIM, (h + 1) * HEAD_DIM)
            keys = kbuf[pl.ds(start, window), cols]
            vals = vbuf[pl.ds(start, window), cols]
            for part in range(0, rep, 4):
                lanes = [
                    slice((h * rep + r) * HEAD_DIM, (h * rep + r + 1) * HEAD_DIM)
                    for r in range(part, part + 4)
                ]
                q = jnp.concatenate(
                    [
                        turn(qbuf[pl.ds(start, TILE), lane].astype(jnp.float32), cosine, sine)
                        for lane in lanes
                    ],
                    0,
                )
                scores = lax.dot_general(
                    q, keys, (((1,), (1,)), ((), ())), preferred_element_type=jnp.float32
                )
                scores = scores.reshape(4, TILE, window)
                scores = jnp.where(mask[None], scores * factor, -1e30)
                expo = jnp.exp2(scores - jnp.max(scores, -1, keepdims=True))
                total = jnp.sum(expo, -1, keepdims=True)
                mixed = jnp.dot(
                    expo.reshape(4 * TILE, window).astype(jnp.bfloat16),
                    vals,
                    preferred_element_type=jnp.float32,
                ).reshape(4, TILE, HEAD_DIM)
                mixed = (mixed / total).astype(jnp.bfloat16)
                for r, lane in enumerate(lanes):
                    obuf[pl.ds(start, TILE), lane] = mixed[r]
        return carry

    lax.fori_loop(0, steps, attend, 0)
    out = pltpu.make_async_copy(obuf, attn_hbm, out_sem)
    out.start()

    for turn_at, whose, action in errands:
        if turn_at >= steps:
            pl.when(whose)(action)

    @pl.when(inner)
    def _():
        raw_slots.wait_send()

    @pl.when(gives_halo)
    def _():
        halos[0].wait_send()

    @pl.when(gives_values)
    def _():
        halos[1].wait_send()

    @pl.when(passes_across)
    def _():
        passed_across.wait_send()

    @pl.when(relays)
    def _():
        for copy in to_relay:
            copy.wait_send()

    @pl.when(passes_relay)
    def _():
        for copy in passed_relay:
            copy.wait_send()

    @pl.when(gives_raw)
    def _():
        raw_k_last.wait_send()

    @pl.when(passes_raw)
    def _():
        to_across.wait_send()
        for copy in passed_raw:
            copy.wait_send()

    blocks = groups * tps
    for i, (_, send, cache) in enumerate(lanes_of):

        def wait_sent(count):
            sent = send.at[pl.ds(0, count)]
            pltpu.make_async_copy(sent, sent, send_sem.at[i]).wait()

        if i == 0:
            few = half * tps - 1
            pl.when(gives_raw)(functools.partial(wait_sent, few))
            pl.when(passes_raw)(functools.partial(wait_sent, blocks + few - 1))
            plain = jnp.logical_not(gives_raw | passes_raw)
            pl.when(plain)(functools.partial(wait_sent, blocks - 1))
        else:
            pl.when(outer)(functools.partial(wait_sent, blocks - 1))
            pl.when(inner)(functools.partial(wait_sent, blocks - 2))
        pltpu.make_async_copy(cache, cache, recv_sem.at[i]).wait()
    out.wait()


def hand_over(*arrays):
    count, pieces = len(arrays), 1

    def copy_kernel(*refs):
        sem = refs[-1]
        copies = []
        for i in range(count):
            piece = arrays[i].shape[0] // pieces
            for j in range(pieces):
                part = pl.ds(j * piece, piece)
                copies.append(
                    pltpu.make_async_copy(
                        refs[i].at[part], refs[count + i].at[part], sem.at[i, j]
                    )
                )
        for copy in copies:
            copy.start()
        for copy in copies:
            copy.wait()

    anywhere = pl.BlockSpec(memory_space=pl.ANY)
    return pl.pallas_call(
        copy_kernel,
        out_shape=tuple(jax.ShapeDtypeStruct(a.shape, a.dtype) for a in arrays),
        in_specs=[anywhere] * count,
        out_specs=(anywhere,) * count,
        scratch_shapes=[pltpu.SemaphoreType.DMA((count, pieces))],
        compiler_params=pltpu.CompilerParams(vmem_limit_bytes=16 * 2**20),
    )(*arrays)


def shards(queries, keys, values, segment_ids, cache_owner):
    rows, width = keys.shape
    groups = lax.axis_size("grp")
    tps = lax.axis_size("tp")
    cap = max(1, rows // (2 * groups))
    if cap % 16 or rows % TILE or rows < 2 * REACH or groups != 8:
        return plain_shards(queries, keys, values, segment_ids, cache_owner)
    anywhere = pl.BlockSpec(memory_space=pl.ANY)
    hbm = pl.BlockSpec(memory_space=pltpu.HBM)
    bf16 = jnp.bfloat16
    table = jnp.asarray(rope_table())
    cache = jax.ShapeDtypeStruct((groups * cap, tps * width), bf16)
    landed = pl.pallas_call(
        functools.partial(kernel, groups, tps, cap),
        out_shape=(jax.ShapeDtypeStruct(queries.shape, bf16), cache, cache),
        in_specs=[hbm] * 6,
        out_specs=(anywhere, anywhere, anywhere),
        scratch_shapes=[
            pltpu.VMEM(queries.shape, bf16),
            pltpu.VMEM((rows, width), bf16),
            pltpu.VMEM((REACH + 2 * rows, width), bf16),
            pltpu.VMEM((REACH + 2 * rows, width), bf16),
            pltpu.VMEM((groups * tps + groups // 2 * tps, cap, width), bf16),
            pltpu.VMEM((groups * tps, cap, width), bf16),
            pltpu.VMEM(queries.shape, bf16),
            pltpu.VMEM((rows, HEAD_DIM), jnp.float32),
            pltpu.VMEM((rows, HEAD_DIM), jnp.float32),
            pltpu.VMEM((1, REACH + rows), jnp.float32),
            pltpu.VMEM((rows, TILE), jnp.float32),
            pltpu.VMEM((2, 1, rows), jnp.int32),
            pltpu.VMEM(table.shape, bf16),
            pltpu.VMEM((1, segment_ids.shape[0]), jnp.int32),
            pltpu.VMEM((1, rows), jnp.int32),
            pltpu.SemaphoreType.DMA((6,)),
            pltpu.SemaphoreType.DMA,
            pltpu.SemaphoreType.DMA((2,)),
            pltpu.SemaphoreType.DMA((2,)),
            pltpu.SemaphoreType.DMA((6,)),
            pltpu.SemaphoreType.DMA((6,)),
            pltpu.SemaphoreType.DMA((6,)),
            pltpu.SemaphoreType.DMA((6,)),
            pltpu.VMEM((2, REACH, width), bf16),
            pltpu.SemaphoreType.DMA((2,)),
            pltpu.SemaphoreType.DMA((2,)),
            pltpu.SemaphoreType.REGULAR,
            pltpu.SemaphoreType.REGULAR,
        ],
        compiler_params=pltpu.CompilerParams(
            collective_id=0, has_side_effects=True, vmem_limit_bytes=40 * 2**20
        ),
    )(
        *(
            pltpu.with_memory_space_constraint(operand, pltpu.HBM)
            for operand in (
                queries,
                keys,
                values,
                table,
                segment_ids.reshape(1, -1),
                cache_owner.reshape(1, -1),
            )
        )
    )
    return hand_over(*landed)


def solution(mesh):
    in_specs = (P("grp", "tp"), P("grp", "tp"), P("grp", "tp"), P(), P("grp", None))
    out_specs = (P("grp", "tp"), P(("grp", "tp"), None), P(("grp", "tp"), None))
    return jax.shard_map(shards, mesh=mesh, in_specs=in_specs, out_specs=out_specs, check_vma=False)
```

```python
import functools
import math

import jax
import jax.numpy as jnp
import ml_dtypes
import numpy as np
from jax import lax
from jax.experimental import pallas as pl
from jax.experimental.pallas import tpu as pltpu
from jax.sharding import PartitionSpec as P

HEAD_DIM = 128
REACH = 256
TILE = 128
MESH = pl.DeviceIdType.MESH
PASS_AT = 0
LATE_AT = 2
GIVE_AT = 2
THEIRS_AT = 2
KEYS_AT = 4


rope_base = 10000.0


def shifted(block, axis, distance):
    devices = range(lax.axis_size(axis))
    route = [(i - distance, i) for i in devices if i - distance in devices]
    return lax.ppermute(block, axis, route)


def earlier_alike(labels):
    alike = labels[:, None] == labels[None, :]
    order = jnp.arange(labels.shape[0], dtype=jnp.int32)
    return jnp.sum((alike & (order[None, :] < order[:, None])).astype(jnp.int32), 1)


def rotate(tensor, places):
    half_dim = tensor.shape[-1] // 2
    inverse = jnp.exp(
        jnp.arange(half_dim, dtype=jnp.float32) * (-2.0 * math.log(rope_base) / tensor.shape[-1])
    )
    angles = places.astype(jnp.float32)[:, None] * inverse[None, :]
    cosine = jnp.cos(angles)[:, None, :]
    sine_part = jnp.sin(angles)[:, None, :]
    first_half = tensor[..., :half_dim].astype(jnp.float32)
    second_half = tensor[..., half_dim:].astype(jnp.float32)
    joined = jnp.concatenate(
        [
            first_half * cosine - second_half * sine_part,
            second_half * cosine + first_half * sine_part,
        ],
        -1,
    )
    return joined.astype(jnp.bfloat16)


def plain_shards(queries, keys, values, segment_ids, cache_owner):
    block_rows = queries.shape[0]
    key_width = keys.shape[1]
    query_heads = queries.shape[1] // HEAD_DIM
    key_heads = key_width // HEAD_DIM
    group_size = query_heads // key_heads
    scale = HEAD_DIM ** (-0.5)
    groups = lax.axis_size("grp")
    tp_count = lax.axis_size("tp")
    group_index = lax.axis_index("grp")
    quarter_cap = max(1, block_rows // (2 * groups))
    own_labels = lax.dynamic_slice_in_dim(segment_ids, group_index * block_rows, block_rows, 0)
    prior_labels = lax.dynamic_slice_in_dim(
        segment_ids, jnp.maximum(group_index - 1, 0) * block_rows, block_rows, 0
    )
    has_prior = group_index > 0
    carried = jnp.where(has_prior, jnp.sum((prior_labels == own_labels[0]).astype(jnp.int32)), 0)
    places = earlier_alike(own_labels) + jnp.where(own_labels == own_labels[0], carried, 0)
    q_rot = rotate(queries.reshape(block_rows, query_heads, HEAD_DIM), places)
    k_rot = rotate(keys.reshape(block_rows, key_heads, HEAD_DIM), places).reshape(
        block_rows, key_width
    )
    prior_keys, prior_values = shifted((k_rot, values), "grp", 1)
    row_index = jnp.arange(block_rows, dtype=jnp.int32)[:, None]
    column_index = jnp.arange(block_rows, dtype=jnp.int32)[None, :]
    local_mask = (own_labels[:, None] == own_labels[None, :]) & (column_index <= row_index)
    prior_mask = (own_labels[:, None] == prior_labels[None, :]) & has_prior

    def head_major(rows_flat):
        return rows_flat.reshape(-1, key_heads, HEAD_DIM).transpose(1, 0, 2)

    local_key_stack = head_major(k_rot)
    local_value_stack = head_major(values)
    prior_key_stack = head_major(prior_keys)
    prior_value_stack = head_major(prior_values)
    joint_mask = jnp.concatenate([prior_mask, local_mask], 1)
    joint_key_stack = jnp.concatenate([prior_key_stack, local_key_stack], 1)
    joint_value_stack = jnp.concatenate([prior_value_stack, local_value_stack], 1)
    query_stack = q_rot.transpose(1, 0, 2)
    head_source = jnp.arange(query_heads, dtype=jnp.int32) // group_size

    def attend(pieces):
        query_rows, source_head = pieces
        key_rows = lax.dynamic_index_in_dim(joint_key_stack, source_head, 0, keepdims=False)
        value_rows = lax.dynamic_index_in_dim(joint_value_stack, source_head, 0, keepdims=False)
        scores = (
            jnp.einsum("td,ud->tu", query_rows, key_rows, preferred_element_type=jnp.float32)
            * scale
        )
        masked = jnp.where(joint_mask, scores, -1e30)
        row_max = jnp.max(masked, -1, keepdims=True)
        expo_terms = jnp.where(joint_mask, jnp.exp(masked - row_max), 0.0)
        weights = (expo_terms / jnp.sum(expo_terms, -1, keepdims=True)).astype(jnp.bfloat16)
        mixed = jnp.dot(weights, value_rows, preferred_element_type=jnp.float32)
        return mixed.astype(jnp.bfloat16)

    head_outputs = lax.map(attend, (query_stack, head_source))
    attention = head_outputs.transpose(1, 0, 2).reshape(block_rows, query_heads * HEAD_DIM)
    owners = cache_owner[:, 0]
    ranks = earlier_alike(owners)
    send_slot = owners * (tp_count * quarter_cap) + ranks
    buffer_rows = groups * tp_count * quarter_cap
    send_keys = jnp.zeros((buffer_rows, key_width), jnp.bfloat16).at[send_slot].set(k_rot)
    send_values = jnp.zeros((buffer_rows, key_width), jnp.bfloat16).at[send_slot].set(values)
    send_keys = send_keys.reshape(groups, tp_count, quarter_cap, key_width)
    send_values = send_values.reshape(groups, tp_count, quarter_cap, key_width)
    middle_keys, middle_values = (
        lax.all_to_all(send_keys, "tp", split_axis=1, concat_axis=3, tiled=True),
        lax.all_to_all(send_values, "tp", split_axis=1, concat_axis=3, tiled=True),
    )
    got_keys, got_values = (
        lax.all_to_all(middle_keys, "grp", split_axis=0, concat_axis=0, tiled=True),
        lax.all_to_all(middle_values, "grp", split_axis=0, concat_axis=0, tiled=True),
    )
    key_cache = got_keys.reshape(groups * quarter_cap, tp_count * key_width)
    value_cache = got_values.reshape(groups * quarter_cap, tp_count * key_width)
    return (attention, key_cache, value_cache)


def rope_table():
    half_dim = HEAD_DIM // 2
    inverse = np.exp(
        np.arange(half_dim, dtype=np.float32) * np.float32(-2.0 * math.log(rope_base) / HEAD_DIM)
    ).astype(np.float32)
    angles = (np.arange(REACH, dtype=np.float32)[:, None] * inverse[None, :]).astype(np.float32)
    cosine = np.cos(angles.astype(np.float64))
    sine = np.sin(angles.astype(np.float64))
    rest = np.concatenate([cosine, cosine, -sine, sine], 1)
    parts = []
    for _ in range(3):
        part = rest.astype(np.float32).astype(ml_dtypes.bfloat16)
        parts.append(part)
        rest = rest - part.astype(np.float64)
    return np.concatenate(parts, 1)


def kernel(
    groups,
    tps,
    cap,
    q_hbm,
    k_hbm,
    v_hbm,
    table_hbm,
    labels_hbm,
    owner_hbm,
    attn_hbm,
    kc_hbm,
    vc_hbm,
    qbuf,
    kraw,
    kbuf,
    vbuf,
    ksend,
    vsend,
    obuf,
    cos_ref,
    sin_ref,
    lab_row,
    lab_col,
    slot_ref,
    table_ref,
    labels_ref,
    owner_ref,
    in_sem,
    out_sem,
    send_sem,
    recv_sem,
    halo_send,
    halo_recv,
    raw_send,
    raw_recv,
    relay_ref,
    relay_send,
    relay_recv,
    ready_sem,
    turn_sem,
):
    rows, width = kraw.shape
    key_heads = width // HEAD_DIM
    q_heads = qbuf.shape[1] // HEAD_DIM
    rep = q_heads // key_heads
    steps = rows // TILE
    window = REACH + TILE
    half = groups // 2
    g = lax.axis_index("grp")
    p = lax.axis_index("tp")
    side = g // half
    y = lax.rem(g, 2)
    first_layer = g < 2
    last_layer = g >= groups - 2
    outer = first_layer | last_layer
    inner = jnp.logical_not(outer)
    partner = jnp.where(side == 0, jnp.minimum(g + 2, groups - 1), jnp.maximum(g - 2, 0))
    own_start = REACH
    partner_start = REACH + rows

    barrier = pltpu.get_barrier_semaphore()

    @pl.when(inner)
    def _():
        pl.semaphore_signal(barrier, inc=1, device_id=(partner, p), device_id_type=MESH)

    @pl.when(inner & (side == 0))
    def _():
        above = jnp.maximum(g - 2, 0)
        pl.semaphore_signal(barrier, inc=1, device_id=(above, p), device_id_type=MESH)

    arrivals = [
        pltpu.make_async_copy(src, dst, in_sem.at[i])
        for i, (src, dst) in enumerate(
            (
                (owner_hbm, owner_ref),
                (labels_hbm, labels_ref),
                (k_hbm, kraw),
                (table_hbm, table_ref),
                (v_hbm, vbuf.at[pl.ds(own_start, rows)]),
                (q_hbm, qbuf),
            )
        )
    ]
    for arrival in arrivals:
        arrival.start()
    owner_in, labels_in, k_in, table_in, v_in, q_in = arrivals

    def greet(i, carry):
        there = groups - 2 + i // tps
        seat = lax.rem(i, tps)

        @pl.when((there != g) | (seat != p))
        def _():
            pl.semaphore_signal(
                barrier, inc=1, device_id=(there, seat), device_id_type=MESH
            )

        return carry

    lax.fori_loop(0, 2 * tps, greet, 0)

    def raw(i, src, dst):
        return pltpu.make_async_remote_copy(
            src_ref=src,
            dst_ref=dst,
            send_sem=raw_send.at[i],
            recv_sem=raw_recv.at[i],
            device_id=(partner, p),
            device_id_type=MESH,
        )

    low, high = rows - REACH, REACH
    raw_v_high = raw(
        0, v_hbm.at[pl.ds(low, high)], vbuf.at[pl.ds(partner_start + low, high)]
    )
    raw_v_low = raw(1, v_hbm.at[pl.ds(0, low)], vbuf.at[pl.ds(partner_start, low)])
    raw_slots = raw(2, slot_ref.at[0], slot_ref.at[1])
    raw_k_high = raw(
        3, kbuf.at[pl.ds(own_start + low, high)], kbuf.at[pl.ds(partner_start + low, high)]
    )
    cut = low - 64
    raw_k_low = raw(4, kbuf.at[pl.ds(own_start, cut)], kbuf.at[pl.ds(partner_start, cut)])
    raw_k_last = raw(
        5,
        kbuf.at[pl.ds(own_start + cut, low - cut)],
        kbuf.at[pl.ds(partner_start + cut, low - cut)],
    )
    gives_raw = g == half - 1
    passes_raw = g == half + 1

    relays = g == 1
    passes_relay = g == half - 1
    to_relay = [
        pltpu.make_async_remote_copy(
            src_ref=src,
            dst_ref=relay_ref.at[i],
            send_sem=relay_send.at[i],
            recv_sem=relay_recv.at[i],
            device_id=(jnp.minimum(g + 2, groups - 1), p),
            device_id_type=MESH,
        )
        for i, src in enumerate((kbuf.at[pl.ds(rows, REACH)], v_hbm.at[pl.ds(low, high)]))
    ]

    @pl.when(jnp.logical_not(last_layer))
    def _():
        pl.semaphore_wait(barrier, 1)

    @pl.when(inner)
    def _():
        raw_v_high.start()

    @pl.when(relays)
    def _():
        to_relay[1].start()

    @pl.when(last_layer)
    def _():
        pl.semaphore_wait(barrier, groups * tps - 1)
        for layer in range(1, groups // 2):
            below = jnp.maximum(g - 2 * layer, 0)
            pl.semaphore_signal(ready_sem, inc=1, device_id=(below, p), device_id_type=MESH)

    owner_in.wait()
    owners = owner_ref[...]
    owner_pad = -(-groups // 16) * 16
    one_hot = (lax.broadcasted_iota(jnp.int32, (owner_pad, rows), 0) == owners).astype(jnp.float32)
    earlier = (
        lax.broadcasted_iota(jnp.int32, (rows, rows), 0)
        < lax.broadcasted_iota(jnp.int32, (rows, rows), 1)
    ).astype(jnp.float32)
    counts = jnp.dot(
        one_hot.astype(jnp.bfloat16),
        earlier.astype(jnp.bfloat16),
        preferred_element_type=jnp.float32,
    )
    ranks = jnp.sum(counts * one_hot, 0, keepdims=True)
    slot_ref[0] = owners * (tps * cap) + ranks.astype(jnp.int32)

    @pl.when(inner)
    def _():
        raw_slots.start()

    def allowed(b):
        start = pl.multiple_of(b * TILE, TILE)
        line = lab_row[:, pl.ds(start, window)]
        col = lab_col[pl.ds(start, TILE), :]
        col = jnp.concatenate([col] * (window // TILE), 1)
        causal = (
            lax.broadcasted_iota(jnp.int32, (TILE, window), 1)
            <= lax.broadcasted_iota(jnp.int32, (TILE, window), 0) + REACH
        )
        return (col == line) & causal

    def turn(x, cosine, sine):
        return (x * cosine + pltpu.roll(x, HEAD_DIM // 2, 1) * sine).astype(jnp.bfloat16)

    labels_in.wait()
    k_in.wait()
    table_in.wait()
    before = pl.multiple_of(jnp.maximum(g * rows - REACH, 0), 128)
    prior = labels_ref[:, pl.ds(before, REACH)].astype(jnp.float32)
    own = labels_ref[:, pl.ds(pl.multiple_of(g * rows, 128), rows)].astype(jnp.float32)
    lab_row[:, :REACH] = jnp.where(jnp.full(prior.shape, g) > 0, prior, -1.0)
    lab_row[:, REACH:] = own
    for b in range(steps):
        line = own[:, b * TILE : (b + 1) * TILE]
        lab_col[pl.ds(b * TILE, TILE), :] = jnp.transpose(jnp.broadcast_to(line, (TILE, TILE)))

    def rotate_keys(b, carry):
        start = pl.multiple_of(b * TILE, TILE)
        place = jnp.sum(allowed(b).astype(jnp.float32), 1, keepdims=True) - 1.0
        pick = lax.broadcasted_iota(jnp.int32, (TILE, REACH), 1) == place.astype(jnp.int32)
        pick = pick.astype(jnp.float32).astype(jnp.bfloat16)
        found = jnp.dot(pick, table_ref[...], preferred_element_type=jnp.float32)
        wide = 2 * HEAD_DIM
        found = found[:, :wide] + found[:, wide : 2 * wide] + found[:, 2 * wide :]
        cosine, sine = found[:, :HEAD_DIM], found[:, HEAD_DIM:]
        cos_ref[pl.ds(start, TILE), :] = cosine
        sin_ref[pl.ds(start, TILE), :] = sine
        for h in range(key_heads):
            cols = slice(h * HEAD_DIM, (h + 1) * HEAD_DIM)
            x = kraw[pl.ds(start, TILE), cols].astype(jnp.float32)
            kbuf[pl.ds(pl.multiple_of(own_start + start, TILE), TILE), cols] = turn(x, cosine, sine)
        return carry

    lax.fori_loop(0, steps, rotate_keys, 0)

    @pl.when(gives_raw)
    def _():
        raw_k_high.start()

    @pl.when(inner)
    def _():
        raw_v_low.start()

    @pl.when(gives_raw)
    def _():
        raw_k_low.start()
        raw_k_last.start()

    @pl.when(relays)
    def _():
        to_relay[0].start()

    v_in.wait()

    @pl.when(jnp.logical_not(last_layer))
    def _():
        pl.semaphore_wait(ready_sem, 1)

    lanes_of = ((kbuf, ksend, kc_hbm), (vbuf, vsend, vc_hbm))
    land_cols = pl.ds(pl.multiple_of(p * width, width), width)

    def deal(unit, i, owner, theirs=False, mine=False):
        buf, send, cache = lanes_of[i]
        source = partner if theirs else g
        first = partner_start if theirs else own_start
        land = cache.at[pl.ds(pl.multiple_of(source * cap, cap), cap), land_cols]
        slots = lax.broadcasted_iota(jnp.int32, (tps * cap, rows), 0) + owner * (tps * cap)
        pick = (slots == slot_ref[int(theirs)]).astype(jnp.float32).astype(jnp.bfloat16)
        got = jnp.dot(pick, buf[pl.ds(first, rows), :], preferred_element_type=jnp.float32)
        send[pl.ds(unit * tps, tps)] = got.astype(jnp.bfloat16).reshape(tps, cap, width)
        for j in range(int(mine), tps):
            quarter = lax.rem(p + j, tps) if mine else j
            pltpu.make_async_remote_copy(
                src_ref=send.at[unit * tps + quarter],
                dst_ref=land,
                send_sem=send_sem.at[i],
                recv_sem=recv_sem.at[i],
                device_id=(owner, quarter),
                device_id_type=MESH,
            ).start()
        if mine:
            pltpu.make_async_copy(send.at[unit * tps + p], land, recv_sem.at[i]).start()

    def deal_far(i):
        def step(s, carry):
            turned = jnp.where(side == 0, 2 - 2 * lax.rem(s, 2) + s // 2, s)
            deal(s, i, (1 - side) * half + turned)
            return carry

        lax.fori_loop(0, half, step, 0)

    def deal_near(i, theirs):
        first = half if not theirs else groups if i == 0 else 0

        def step(s, carry):
            deal(first + s, i, side * half + lax.rem(g + s + 1, half), theirs)
            return carry

        lax.fori_loop(0, half - 1, step, 0)
        deal(first + half - 1, i, g, theirs, True)

    def halo(src, buf, i, to):
        return pltpu.make_async_remote_copy(
            src_ref=src,
            dst_ref=buf.at[pl.ds(0, REACH)],
            send_sem=halo_send.at[i],
            recv_sem=halo_recv.at[i],
            device_id=(to, p),
            device_id_type=MESH,
        )

    following = jnp.minimum(g + 1, groups - 1)
    preceding = jnp.maximum(g - 1, 0)
    gives_halo = (g != 1) & (g != half - 1) & (g < groups - 1)
    bufs = (kbuf, vbuf)
    halos = [halo(buf.at[pl.ds(rows, REACH)], buf, i, following) for i, buf in enumerate(bufs)]
    passed_relay = [halo(relay_ref.at[i], buf, 2 + i, preceding) for i, buf in enumerate(bufs)]
    passed_raw = [
        halo(buf.at[pl.ds(2 * rows, REACH)], buf, 2 + i, preceding)
        for i, buf in enumerate(bufs)
    ]
    gets_passed = (g == 2) | (g == half)
    gives_values = gives_halo & (g != half + 1)
    passes_across = g == half
    gets_across = g == half + 2
    to_across = pltpu.make_async_remote_copy(
        src_ref=vbuf.at[pl.ds(rows, REACH)],
        dst_ref=relay_ref.at[1],
        send_sem=relay_send.at[1],
        recv_sem=relay_recv.at[1],
        device_id=(preceding, p),
        device_id_type=MESH,
    )
    passed_across = halo(relay_ref.at[1], vbuf, 4, jnp.minimum(g + 2, groups - 1))

    @pl.when(gives_halo)
    def _():
        halos[0].start()

    @pl.when(gives_values)
    def _():
        halos[1].start()

    @pl.when(passes_raw)
    def _():
        to_across.start()

    late_far = g == 1
    soon_far = outer & jnp.logical_not(late_far)

    deal_near(1, False)

    @pl.when(soon_far)
    def _():
        deal_far(1)

    deal_near(0, False)

    @pl.when(soon_far)
    def _():
        deal_far(0)

    @pl.when(inner & jnp.logical_not(gives_raw))
    def _():
        raw_v_high.wait_send()
        raw_v_low.wait_send()

    @pl.when(inner & jnp.logical_not(gives_raw))
    def _():
        deal_far(0)

    @pl.when(g == 0)
    def _():
        kbuf[:REACH, :] = jnp.zeros((REACH, width), jnp.bfloat16)
        vbuf[:REACH, :] = jnp.zeros((REACH, width), jnp.bfloat16)

    q_in.wait()

    def pass_relay():
        for copy in to_relay:
            copy.wait_recv()
        for copy in passed_relay:
            copy.start()

    def pass_across():
        to_across.wait_recv()
        passed_across.start()

    def pass_raw():
        raw_k_high.wait_recv()
        raw_v_high.wait_recv()
        for copy in passed_raw:
            copy.start()

    def deal_their_values():
        @pl.when(jnp.logical_not(passes_raw))
        def _():
            raw_v_high.wait_recv()

        raw_v_low.wait_recv()
        raw_slots.wait_recv()
        deal_near(1, True)

    def deal_their_keys():
        raw_k_low.wait_recv()
        raw_k_last.wait_recv()
        deal_near(0, True)

    def give_turn():
        raw_v_high.wait_send()
        raw_v_low.wait_send()
        raw_k_high.wait_send()
        raw_k_low.wait_send()
        above = jnp.maximum(g - 2, 0)
        pl.semaphore_signal(turn_sem, inc=1, device_id=(above, p), device_id_type=MESH)

    def late_deal():
        pl.semaphore_wait(turn_sem, 1)
        deal_far(1)
        deal_far(0)

    errands = (
        (GIVE_AT, gives_raw, give_turn),
        (LATE_AT, late_far, late_deal),
        (PASS_AT, passes_relay, pass_relay),
        (PASS_AT, passes_raw, pass_raw),
        (PASS_AT, passes_across, pass_across),
        (THEIRS_AT, inner, deal_their_values),
        (KEYS_AT, passes_raw, deal_their_keys),
    )

    factor = HEAD_DIM**-0.5 * math.log2(math.e)
    ahead = steps - REACH // TILE

    def attend(it, carry):
        b = lax.rem(it + REACH // TILE, steps)
        start = pl.multiple_of(b * TILE, TILE)

        for turn_at, whose, action in errands:
            if turn_at < steps:
                pl.when((it == turn_at) & whose)(action)

        @pl.when((it == ahead) & (g > 0) & jnp.logical_not(gets_passed))
        def _():
            halos[0].wait_recv()

        @pl.when((it == ahead) & (g > 0) & jnp.logical_not(gets_passed | gets_across))
        def _():
            halos[1].wait_recv()

        @pl.when((it == ahead) & gets_across)
        def _():
            passed_across.wait_recv()

        @pl.when((it == ahead) & gets_passed)
        def _():
            for copy in passed_raw:
                copy.wait_recv()

        mask = allowed(b)
        cosine = cos_ref[pl.ds(start, TILE), :]
        sine = sin_ref[pl.ds(start, TILE), :]
        for h in range(key_heads):
            cols = slice(h * HEAD_DIM, (h + 1) * HEAD_DIM)
            keys = kbuf[pl.ds(start, window), cols]
            vals = vbuf[pl.ds(start, window), cols]
            for part in range(0, rep, 4):
                lanes = [
                    slice((h * rep + r) * HEAD_DIM, (h * rep + r + 1) * HEAD_DIM)
                    for r in range(part, part + 4)
                ]
                q = jnp.concatenate(
                    [
                        turn(qbuf[pl.ds(start, TILE), lane].astype(jnp.float32), cosine, sine)
                        for lane in lanes
                    ],
                    0,
                )
                scores = lax.dot_general(
                    q, keys, (((1,), (1,)), ((), ())), preferred_element_type=jnp.float32
                )
                scores = scores.reshape(4, TILE, window)
                scores = jnp.where(mask[None], scores * factor, -1e30)
                expo = jnp.exp2(scores - jnp.max(scores, -1, keepdims=True))
                total = jnp.sum(expo, -1, keepdims=True)
                mixed = jnp.dot(
                    expo.reshape(4 * TILE, window).astype(jnp.bfloat16),
                    vals,
                    preferred_element_type=jnp.float32,
                ).reshape(4, TILE, HEAD_DIM)
                mixed = (mixed / total).astype(jnp.bfloat16)
                for r, lane in enumerate(lanes):
                    obuf[pl.ds(start, TILE), lane] = mixed[r]
        return carry

    lax.fori_loop(0, steps, attend, 0)
    out = pltpu.make_async_copy(obuf, attn_hbm, out_sem)
    out.start()

    for turn_at, whose, action in errands:
        if turn_at >= steps:
            pl.when(whose)(action)

    @pl.when(inner)
    def _():
        raw_slots.wait_send()

    @pl.when(gives_halo)
    def _():
        halos[0].wait_send()

    @pl.when(gives_values)
    def _():
        halos[1].wait_send()

    @pl.when(passes_across)
    def _():
        passed_across.wait_send()

    @pl.when(relays)
    def _():
        for copy in to_relay:
            copy.wait_send()

    @pl.when(passes_relay)
    def _():
        for copy in passed_relay:
            copy.wait_send()

    @pl.when(gives_raw)
    def _():
        raw_k_last.wait_send()

    @pl.when(passes_raw)
    def _():
        to_across.wait_send()
        for copy in passed_raw:
            copy.wait_send()

    blocks = groups * tps
    for i, (_, send, cache) in enumerate(lanes_of):

        def wait_sent(count):
            sent = send.at[pl.ds(0, count)]
            pltpu.make_async_copy(sent, sent, send_sem.at[i]).wait()

        if i == 0:
            few = half * tps - 1
            pl.when(gives_raw)(functools.partial(wait_sent, few))
            pl.when(passes_raw)(functools.partial(wait_sent, blocks + few - 1))
            plain = jnp.logical_not(gives_raw | passes_raw)
            pl.when(plain)(functools.partial(wait_sent, blocks - 1))
        else:
            pl.when(outer)(functools.partial(wait_sent, blocks - 1))
            pl.when(inner)(functools.partial(wait_sent, blocks - 2))
        pltpu.make_async_copy(cache, cache, recv_sem.at[i]).wait()
    out.wait()


def hand_over(*arrays):
    count, pieces = len(arrays), 1

    def copy_kernel(*refs):
        sem = refs[-1]
        copies = []
        for i in range(count):
            piece = arrays[i].shape[0] // pieces
            for j in range(pieces):
                part = pl.ds(j * piece, piece)
                copies.append(
                    pltpu.make_async_copy(
                        refs[i].at[part], refs[count + i].at[part], sem.at[i, j]
                    )
                )
        for copy in copies:
            copy.start()
        for copy in copies:
            copy.wait()

    anywhere = pl.BlockSpec(memory_space=pl.ANY)
    return pl.pallas_call(
        copy_kernel,
        out_shape=tuple(jax.ShapeDtypeStruct(a.shape, a.dtype) for a in arrays),
        in_specs=[anywhere] * count,
        out_specs=(anywhere,) * count,
        scratch_shapes=[pltpu.SemaphoreType.DMA((count, pieces))],
        compiler_params=pltpu.CompilerParams(vmem_limit_bytes=16 * 2**20),
    )(*arrays)


def shards(queries, keys, values, segment_ids, cache_owner):
    rows, width = keys.shape
    groups = lax.axis_size("grp")
    tps = lax.axis_size("tp")
    cap = max(1, rows // (2 * groups))
    if cap % 16 or rows % TILE or rows < 2 * REACH or groups != 8:
        return plain_shards(queries, keys, values, segment_ids, cache_owner)
    anywhere = pl.BlockSpec(memory_space=pl.ANY)
    hbm = pl.BlockSpec(memory_space=pltpu.HBM)
    bf16 = jnp.bfloat16
    table = jnp.asarray(rope_table())
    cache = jax.ShapeDtypeStruct((groups * cap, tps * width), bf16)
    landed = pl.pallas_call(
        functools.partial(kernel, groups, tps, cap),
        out_shape=(jax.ShapeDtypeStruct(queries.shape, bf16), cache, cache),
        in_specs=[hbm] * 6,
        out_specs=(anywhere, anywhere, anywhere),
        scratch_shapes=[
            pltpu.VMEM(queries.shape, bf16),
            pltpu.VMEM((rows, width), bf16),
            pltpu.VMEM((REACH + 2 * rows, width), bf16),
            pltpu.VMEM((REACH + 2 * rows, width), bf16),
            pltpu.VMEM((groups * tps + groups // 2 * tps, cap, width), bf16),
            pltpu.VMEM((groups * tps, cap, width), bf16),
            pltpu.VMEM(queries.shape, bf16),
            pltpu.VMEM((rows, HEAD_DIM), jnp.float32),
            pltpu.VMEM((rows, HEAD_DIM), jnp.float32),
            pltpu.VMEM((1, REACH + rows), jnp.float32),
            pltpu.VMEM((rows, TILE), jnp.float32),
            pltpu.VMEM((2, 1, rows), jnp.int32),
            pltpu.VMEM(table.shape, bf16),
            pltpu.VMEM((1, segment_ids.shape[0]), jnp.int32),
            pltpu.VMEM((1, rows), jnp.int32),
            pltpu.SemaphoreType.DMA((6,)),
            pltpu.SemaphoreType.DMA,
            pltpu.SemaphoreType.DMA((2,)),
            pltpu.SemaphoreType.DMA((2,)),
            pltpu.SemaphoreType.DMA((6,)),
            pltpu.SemaphoreType.DMA((6,)),
            pltpu.SemaphoreType.DMA((6,)),
            pltpu.SemaphoreType.DMA((6,)),
            pltpu.VMEM((2, REACH, width), bf16),
            pltpu.SemaphoreType.DMA((2,)),
            pltpu.SemaphoreType.DMA((2,)),
            pltpu.SemaphoreType.REGULAR,
            pltpu.SemaphoreType.REGULAR,
        ],
        compiler_params=pltpu.CompilerParams(
            collective_id=0, has_side_effects=True, vmem_limit_bytes=40 * 2**20
        ),
    )(
        *(
            pltpu.with_memory_space_constraint(operand, pltpu.HBM)
            for operand in (
                queries,
                keys,
                values,
                table,
                segment_ids.reshape(1, -1),
                cache_owner.reshape(1, -1),
            )
        )
    )
    return hand_over(*landed)


def solution(mesh):
    in_specs = (P("grp", "tp"), P("grp", "tp"), P("grp", "tp"), P(), P("grp", None))
    out_specs = (P("grp", "tp"), P(("grp", "tp"), None), P(("grp", "tp"), None))
    return jax.shard_map(shards, mesh=mesh, in_specs=in_specs, out_specs=out_specs, check_vma=False)
```
